512 devices in a mesh: page: 32 (over z, core), query: 8 (over y, x_hi), head: 2 (over x_lo).
Axes of the slice: x: 4 (x_hi: 2, x_lo: 2; x = x_hi * 2 + x_lo), y: 4, z: 16, core: 2. Of those that a mesh axis runs over, the one named last changes fastest.
Arguments:
- queries: float32 [8, 2048, 128], P('head', 'query'), may hold values from -40 to 40
- compact_keys: float32 [8, 8192, 128], P('head', 'page'), may hold values from -4 to 4
- compact_values: float32 [8, 8192, 128], P('head', 'page'), may hold values from -6 to 6
- slot_bias: float32 [8, 8192], P('head', 'page'), may hold values from -0.25 to 0.25
- targets: float32 [8, 2048, 128], P('head', 'query'), may hold values from -4 to 4
- positions: int32 [8, 2048], P('head', 'query'), may hold values from 0 to 1048575
- assignment: int32 [32], replicated, may hold values from 0 to 31, as said below
Outputs:
- new_keys: float32 [8, 8192, 128], P('head', 'page')
- new_values: float32 [8, 8192, 128], P('head', 'page')
- new_bias: float32 [8, 8192], P('head', 'page')
The draws below stay inside these ranges and needn't reach their ends.
Inputs may be any that keep to these rules, and one draw needn't show every extreme that they name: `assignment`: a permutation: every page 0 to 31 is held by exactly one page-axis block.
All inputs are finite; a program needn't handle non-finite values.
Results may differ from the reference program's by a relative error of at most 0.0003.
Values sent between devices are 32-bit elements; how exact they have to be, the bound alone decides.
A program may use at most 64 MiB of HBM per device.

```python
import math
import jax
import jax.numpy as jnp
from jax import lax

KV_HEADS = 8
HD = 128
SLOT_DEV = 256
STEPS = 2
PAGE_LEN = 32768
SLOTS = 8192
QN = 2048
CONTEXT = 1048576
N_PAGE = 32


def common_draw(key):
    assign_order = jax.random.permutation(jax.random.fold_in(key, 11), N_PAGE).astype(jnp.int32)
    key_seed = jax.random.fold_in(key, 12)
    query_seed = jax.random.fold_in(key, 13)
    slot_keys = jax.random.truncated_normal(key_seed, -4.0, 4.0, (KV_HEADS, SLOTS, HD), jnp.float32)
    query_rows = jax.random.truncated_normal(query_seed, -4.0, 4.0, (KV_HEADS, QN, HD), jnp.float32)
    return (assign_order, slot_keys, query_rows)


def draw_assignment(key, part):
    return common_draw(key)[0]


def draw_compact_keys(key, part):
    return common_draw(key)[1]


def draw_queries(key, part):
    return common_draw(key)[2]


def with_ends(result, key, least, largest):
    place = [jax.random.randint(jax.random.fold_in(key, axis), (), 0, length) for axis, length in enumerate(result.shape)]
    main_axis = result.shape.index(max(result.shape))
    next_to = place[:main_axis] + [(place[main_axis] + 1) % result.shape[main_axis]] + place[main_axis + 1:]
    return result.at[tuple(place)].set(least).at[tuple(next_to)].set(largest)


def level_of(own_key, shape, shards, smallest, top_value):
    level, own = 1.0, jax.random.fold_in(own_key, 6)
    for axis_at, parts in shards:
        draws = jnp.exp(jax.random.uniform(jax.random.fold_in(own, axis_at), (parts,), jnp.float32, smallest / len(shards), top_value / len(shards)))
        level = level * jnp.repeat(draws, shape[axis_at] // parts).reshape([-1 if axis == axis_at else 1 for axis in range(len(shape))])
    return level


def gaussian(own_key, dims, deviation, most, shards=(), kind=jnp.bfloat16):
    level = level_of(own_key, dims, shards, -0.22, 0.18) if shards else 1.0
    result = jax.random.normal(own_key, dims, jnp.float32) * deviation * level
    return jnp.minimum(jnp.maximum(result, -most), most).astype(kind)


def setup_inputs(seed: int = 0) -> dict:
    key_of = jax.random.split(jax.random.key(seed), 8)
    return {
        "queries": draw_queries(jax.random.fold_in(key_of[7], 71), 0),
        "compact_keys": draw_compact_keys(jax.random.fold_in(key_of[7], 71), 0),
        "compact_values": gaussian(key_of[2], (KV_HEADS, SLOTS, HD), 1.0, 6.0, ((0, 2), (1, 32)), jnp.float32),
        "slot_bias": jnp.clip(jax.random.uniform(key_of[3], (KV_HEADS, SLOTS), jnp.float32, -0.25, 0.25) * level_of(key_of[3], (KV_HEADS, SLOTS), ((0, 2), (1, 32)), -0.4, 0.0), -0.25, 0.25),
        "targets": gaussian(key_of[4], (KV_HEADS, QN, HD), 0.5, 4.0, ((0, 2), (1, 8)), jnp.float32),
        "positions": with_ends(jax.random.randint(key_of[5], (KV_HEADS, QN), 0, CONTEXT), jax.random.fold_in(key_of[5], 1), 0, CONTEXT - 1).astype(jnp.int32),
        "assignment": draw_assignment(jax.random.fold_in(key_of[7], 71), 0),
    }


MASKED = -1e+30
EPSILON = 1e-06
RATE_KEYS = 0.05
RATE_VALUES = 0.05
RATE_BIAS = 0.2
HIGHEST = lax.Precision.HIGHEST

def reference(queries, compact_keys, compact_values, slot_bias, targets, positions, assignment):
    score_scale = 1.0 / math.sqrt(HD)
    slot_page = assignment[jnp.arange(SLOTS, dtype=jnp.int32) // SLOT_DEV]

    def head_gradients(inputs):
        query_rows, key_rows, value_rows, bias_row, target_rows, position_row = inputs
        visible = slot_page[None, :] <= (position_row // PAGE_LEN)[:, None]
        scores = jnp.dot(query_rows, key_rows.T, precision=HIGHEST) * score_scale + bias_row[None, :]
        scores = jnp.where(visible, scores, MASKED)
        row_max = lax.optimization_barrier(jnp.max(scores, axis=1))
        weights = jnp.where(visible, jnp.exp(scores - row_max[:, None]), 0.0)
        row_total = lax.optimization_barrier(jnp.sum(weights, axis=1))
        attention = weights / row_total[:, None]
        output = jnp.dot(attention, value_rows, precision=HIGHEST)
        residual = output - target_rows
        grad_values = jnp.dot(attention.T, residual, precision=HIGHEST)
        row_delta = lax.optimization_barrier(jnp.sum(residual * output, axis=1))
        grad_probs = jnp.dot(residual, value_rows.T, precision=HIGHEST)
        grad_scores = attention * (grad_probs - row_delta[:, None])
        grad_bias = lax.optimization_barrier(jnp.sum(grad_scores, axis=0))
        grad_keys = jnp.dot(grad_scores.T, query_rows, precision=HIGHEST) * score_scale
        return (grad_keys, grad_values, grad_bias)
    key_state, value_state, bias_state = (compact_keys, compact_values, slot_bias)
    for repeat in range(STEPS):
        grad_keys, grad_values, grad_bias = lax.map(head_gradients, (queries, key_state, value_state, bias_state, targets, positions))
        rms_keys = jnp.sqrt(jnp.sum(grad_keys * grad_keys) / (KV_HEADS * SLOTS * HD) + EPSILON)
        rms_values = jnp.sqrt(jnp.sum(grad_values * grad_values) / (KV_HEADS * SLOTS * HD) + EPSILON)
        rms_bias = jnp.sqrt(jnp.sum(grad_bias * grad_bias) / (KV_HEADS * SLOTS) + EPSILON)
        key_state = key_state - RATE_KEYS * grad_keys / rms_keys
        value_state = value_state - RATE_VALUES * grad_values / rms_values
        bias_state = bias_state - RATE_BIAS * grad_bias / rms_bias
    return (key_state, value_state, bias_state)
```

```python
import functools
import math

import jax
import jax.numpy as jnp
from jax import lax
from jax.experimental import pallas as pl
from jax.experimental.pallas import tpu as pltpu
from jax.sharding import PartitionSpec as P

STEPS = 2
PAGE_SHIFT = 15
MASKED = -1e30
EPSILON = 1e-06
RATE_KEYS = 0.05
RATE_VALUES = 0.05
RATE_BIAS = 0.2
HIGHEST = lax.Precision.HIGHEST
MESH = pl.DeviceIdType.MESH
F32 = jnp.float32


def dot(a, b, ca, cb):
    return lax.dot_general(
        a, b, (((ca,), (cb,)), ((), ())), precision=HIGHEST, preferred_element_type=F32
    )


def far_first(n):
    return sorted(range(1, n), key=lambda i: (-min(i, n - i), i))


def kernel(
    nz, ny, nx, q_in, k_in, v_in, b_in, t_in, pos_in, page_in, k_out, v_out, b_out,
    qg, tp, tg, st_s, po, pin, zs, zr, rt, gl, gp_r, gbl, gbp, og, ogb, s1s, s1, s2s, s2,
    kc, vc,
    q_ss, q_rs, t_ss, t_rs, c_ss, c_rs, z_ss, z_rs, a_ss, a_rs, f_ss, f_rs, p_ss, p_rs,
    o_ss, o_rs, ob_ss, ob_rs, s1_ss, s1_rs, s2_ss, s2_rs,
):
    qb, d = q_in.shape[1:]
    slots = k_in.shape[1]
    nb = ny // 2
    hq = nb * qb
    dr = d // nz
    kr = hq // 128
    ng = ny * nx * 2
    scale = 1.0 / math.sqrt(d)
    slot_total = ny * nx * slots * nz * 2
    entry_count = slot_total * d

    page = lax.axis_index("page")
    z, core = page // 2, lax.rem(page, 2)
    g = lax.axis_index("query")
    y, xh = g // 2, lax.rem(g, 2)
    xl = lax.axis_index("head")
    gi = (y * nx + xl) * 2 + core

    def at_z(i):
        other = lax.rem(z + i, nz)
        return other, {"page": other * 2 + core}

    def at_y(i):
        other = lax.rem(y + i, ny)
        return other, {"query": other * 2 + xh}

    def at_g(i):
        other = lax.rem(gi + i, ng)
        oc = lax.rem(other, 2)
        ox = lax.rem(other // 2, nx)
        oy = other // (2 * nx)
        return other, {"page": z * 2 + oc, "query": oy * 2 + xh, "head": ox}

    other_core = {"page": z * 2 + 1 - core}
    pair = {"query": y * 2 + 1 - xh}

    barrier = pltpu.get_barrier_semaphore()
    for i in range(1, ng):
        pl.semaphore_signal(barrier, inc=1, device_id=at_g(i)[1], device_id_type=MESH)
    for i in range(1, nz):
        pl.semaphore_signal(barrier, inc=1, device_id=at_z(i)[1], device_id_type=MESH)
    pl.semaphore_signal(barrier, inc=1, device_id=pair, device_id_type=MESH)

    pending = []

    def send(src, dst, ss, rs, dev):
        copy = pltpu.make_async_remote_copy(
            src_ref=src, dst_ref=dst, send_sem=ss, recv_sem=rs, device_id=dev, device_id_type=MESH
        )
        copy.start()
        pending.append(copy)

    def arrive(dst, ss, rs, dev):
        pltpu.make_async_remote_copy(
            src_ref=dst, dst_ref=dst, send_sem=ss, recv_sem=rs, device_id=dev, device_id_type=MESH
        ).wait_recv()

    pages = (pos_in[...] >> PAGE_SHIFT).astype(F32)
    pick = (
        lax.broadcasted_iota(jnp.int32, (dr, d), 1)
        == lax.broadcasted_iota(jnp.int32, (dr, d), 0) + z * dr
    ).astype(F32)
    for h in range(ny):
        tp[h, :dr, :] = dot(pick, t_in[h], 1, 1)
        tp[h, dr:, :] = jnp.broadcast_to(pages[h : h + 1], (8, qb))
    qg[y] = q_in[y]
    tg[y] = tp[y]
    kc[...] = k_in[y]
    vc[...] = v_in[y]
    my_page = page_in[page].astype(F32)
    row_of = lax.broadcasted_iota(jnp.int32, (ny, slots), 0)
    bias_row = jnp.sum(jnp.where(row_of == y, b_in[...], 0.0), axis=0, keepdims=True)

    pl.semaphore_wait(barrier, ng - 1 + nz - 1 + 1)

    for i in range(1, ny):
        other, dev = at_y(i)
        send(q_in.at[other], qg.at[y], q_ss.at[other], q_rs.at[y], dev)
        send(tp.at[other], tg.at[y], t_ss.at[other], t_rs.at[y], dev)

    def column(row):
        return jnp.transpose(jnp.broadcast_to(row, (128, slots)))[:, :1]

    def stack_rows(rows, height, width):
        at = lax.broadcasted_iota(jnp.int32, (height, width), 0)
        tile = jnp.zeros((height, width), F32)
        for r, row in enumerate(rows):
            tile = jnp.where(at == r, jnp.broadcast_to(row, (height, width)), tile)
        return tile

    rates = []
    for step in range(STEPS):
        keys, values = kc[...], vc[...]
        bias_col = column(bias_row)
        for i in range(ny):
            blk = lax.rem(y + i, ny)
            if step == 0 and i > 0:
                dev = at_y(i)[1]
                arrive(qg.at[blk], q_ss.at[blk], q_rs.at[blk], dev)
                arrive(tg.at[blk], t_ss.at[blk], t_rs.at[blk], dev)
            seen = my_page <= tg[blk, dr : dr + 1, :]
            scores = dot(keys, qg[blk], 1, 1) * scale + bias_col
            scores = jnp.where(seen, scores, MASKED)
            st_s[blk] = scores
            top = jnp.max(scores, axis=0, keepdims=True)
            weights = jnp.where(seen, jnp.exp(scores - top), 0.0)
            po[step, blk, :d, :] = dot(values, weights, 0, 0)
            total = jnp.sum(weights, axis=0, keepdims=True)
            po[step, blk, d:, :] = stack_rows([top, total], 8, qb)

        give = pl.ds((1 - core) * nb, nb)
        send(po.at[step, give], pin.at[step], c_ss.at[step], c_rs.at[step], other_core)
        arrive(pin.at[step], c_ss.at[step], c_rs.at[step], other_core)
        tops, totals = [], []
        for j in range(nb):
            mine, theirs = po[step, core * nb + j], pin[step, j]
            m0, m1 = mine[d : d + 1], theirs[d : d + 1]
            top = jnp.maximum(m0, m1)
            f0, f1 = jnp.exp(m0 - top), jnp.exp(m1 - top)
            zs[step, :, :, j * qb : (j + 1) * qb] = (mine[:d] * f0 + theirs[:d] * f1).reshape(nz, dr, qb)
            total = mine[d + 1 : d + 2] * f0 + theirs[d + 1 : d + 2] * f1
            for a in range(0, qb, 128):
                tops.append(top[:, a : a + 128])
                totals.append(total[:, a : a + 128])
        tile = stack_rows(tops + totals, dr, 128)
        zs[step, :, :, hq:] = jnp.broadcast_to(tile[None], (nz, dr, 128))

        for i in far_first(nz):
            other, dev = at_z(i)
            send(zs.at[step, other], zr.at[step, z], z_ss.at[step, other], z_rs.at[step, z], dev)
        zr[step, z] = zs[step, z]
        for i in range(1, nz):
            other, dev = at_z(i)
            arrive(zr.at[step, other], z_ss.at[step, other], z_rs.at[step, other], dev)
        deltas, lses = [], []
        for r in range(kr):
            lanes = slice(r * 128, (r + 1) * 128)
            m_all = zr[step, :, r, hq:]
            l_all = zr[step, :, kr + r, hq:]
            top = jnp.max(m_all, axis=0, keepdims=True)
            f_all = jnp.exp(m_all - top)
            total = jnp.sum(f_all * l_all, axis=0, keepdims=True)
            output = jnp.sum(zr[step, :, :, lanes] * f_all[:, None, :], axis=0) / total
            blk, off = core * nb + (r * 128) // qb, (r * 128) % qb
            residual = output - tg[blk, :dr, off : off + 128]
            rt[step, core, z, :, lanes] = residual
            deltas.append(jnp.sum(residual * output, axis=0, keepdims=True))
            lses.append(top + jnp.log(total))
        rt[step, core, z, :, hq:] = stack_rows(deltas + lses, dr, 128)

        own = rt.at[step, core, z]
        for i in far_first(nz):
            other, dev = at_z(i)
            send(own, own, a_ss.at[step, other], a_rs.at[step, z], dev)
        send(own, own, f_ss.at[step, z], f_rs.at[step, z], other_core)
        for i in reversed(far_first(nz)):
            other, dev = at_z(i)
            there = rt.at[step, core, other]
            arrive(there, a_ss.at[step, other], a_rs.at[step, other], dev)
            send(there, there, f_ss.at[step, other], f_rs.at[step, other], other_core)

        grad_keys = jnp.zeros((slots, d), F32)
        grad_values = jnp.zeros((slots, d), F32)
        grad_bias = jnp.zeros((8, slots), F32)
        for late in range(2):
            half = core if late == 0 else 1 - core
            if late:
                for i in range(nz):
                    other = lax.rem(z + i, nz)
                    there = rt.at[step, half, other]
                    arrive(there, f_ss.at[step, other], f_rs.at[step, other], other_core)
            for j in range(nb):
                blk = half * nb + j
                lses, deltas = [], []
                for a in range(0, qb, 128):
                    r = (j * qb + a) // 128
                    deltas.append(jnp.sum(rt[step, half, :, r, hq:], axis=0, keepdims=True))
                    lses.append(rt[step, half, 0, kr + r : kr + r + 1, hq:])
                delta, lse = jnp.concatenate(deltas, axis=1), jnp.concatenate(lses, axis=1)
                residual = rt[step, half, :, :, j * qb : (j + 1) * qb].reshape(d, qb)
                attention = jnp.exp(st_s[blk] - lse)
                grad_values += dot(attention, residual, 1, 1)
                grad_scores = attention * (dot(values, residual, 1, 0) - delta)
                grad_keys += dot(grad_scores, qg[blk], 1, 0)
                grad_bias += dot(jnp.ones((8, qb), F32), grad_scores, 1, 1)
        gl[step, 0] = grad_keys * scale
        gl[step, 1] = grad_values
        gbl[step] = grad_bias

        send(gl.at[step], gp_r.at[step], p_ss.at[step, 0], p_rs.at[step, 0], pair)
        send(gbl.at[step], gbp.at[step], p_ss.at[step, 1], p_rs.at[step, 1], pair)
        arrive(gp_r.at[step], p_ss.at[step, 0], p_rs.at[step, 0], pair)
        arrive(gbp.at[step], p_ss.at[step, 1], p_rs.at[step, 1], pair)
        grad_keys = gl[step, 0] + gp_r[step, 0]
        grad_values = gl[step, 1] + gp_r[step, 1]
        grad_bias = gbl[step] + gbp[step]
        bias_grad_row = grad_bias[:1]
        squares = jnp.sum(bias_grad_row * bias_grad_row, axis=1, keepdims=True) / 128
        s1s[step] = stack_rows(
            [
                jnp.sum(grad_keys * grad_keys, axis=0, keepdims=True),
                jnp.sum(grad_values * grad_values, axis=0, keepdims=True),
                jnp.broadcast_to(squares, (1, 128)),
            ],
            8,
            128,
        )
        for i in range(1, ng):
            other, dev = at_g(i)
            send(s1s.at[step], s1.at[step, gi], s1_ss.at[step, other], s1_rs.at[step, gi], dev)
        s1[step, gi] = s1s[step]
        og[step, y, 0] = grad_keys
        og[step, y, 1] = grad_values
        ogb[step, y] = grad_bias
        for i in range(1, ny):
            other, dev = at_y(i)
            mine = og.at[step, y]
            send(mine, mine, o_ss.at[step, other], o_rs.at[step, y], dev)
            mine = ogb.at[step, y]
            send(mine, mine, ob_ss.at[step, other], ob_rs.at[step, y], dev)
        for i in range(1, ng):
            other, dev = at_g(i)
            arrive(s1.at[step, other], s1_ss.at[step, other], s1_rs.at[step, other], dev)
        s2s[step] = jnp.sum(s1[step], axis=0)
        for i in far_first(nz):
            other, dev = at_z(i)
            send(s2s.at[step], s2.at[step, z], s2_ss.at[step, other], s2_rs.at[step, z], dev)
        s2[step, z] = s2s[step]
        for i in range(1, nz):
            other, dev = at_z(i)
            arrive(s2.at[step, other], s2_ss.at[step, other], s2_rs.at[step, other], dev)
        sums = jnp.sum(jnp.sum(s2[step], axis=0), axis=1, keepdims=True)
        rate_keys = RATE_KEYS / jnp.sqrt(sums[0:1] / entry_count + EPSILON)
        rate_values = RATE_VALUES / jnp.sqrt(sums[1:2] / entry_count + EPSILON)
        rate_bias = RATE_BIAS / jnp.sqrt(sums[2:3] / slot_total + EPSILON)
        rates.append((rate_keys, rate_values, rate_bias))
        if step < STEPS - 1:
            kc[...] = keys - rate_keys * grad_keys
            vc[...] = values - rate_values * grad_values
            bias_row = bias_row - rate_bias * bias_grad_row

    for step in range(STEPS):
        for i in range(1, ny):
            other, dev = at_y(i)
            arrive(og.at[step, other], o_ss.at[step, other], o_rs.at[step, other], dev)
            arrive(ogb.at[step, other], ob_ss.at[step, other], ob_rs.at[step, other], dev)
    for h in range(ny):
        new_keys, new_values, new_bias = k_in[h], v_in[h], b_in[h : h + 1]
        for step in range(STEPS):
            rate_keys, rate_values, rate_bias = rates[step]
            new_keys = new_keys - rate_keys * og[step, h, 0]
            new_values = new_values - rate_values * og[step, h, 1]
            new_bias = new_bias - rate_bias * ogb[step, h, :1]
        k_out[h] = new_keys
        v_out[h] = new_values
        b_out[h : h + 1] = new_bias
    for copy in pending:
        copy.wait_send()


def per_device(nz, ny, nx, queries, compact_keys, compact_values, slot_bias, targets, positions, assignment):
    qb, d = queries.shape[1:]
    slots = compact_keys.shape[1]
    nb = ny // 2
    hq, dr, ng = nb * qb, d // nz, ny * nx * 2
    sems = [
        (ny,), (ny,), (ny,), (ny,), (STEPS,), (STEPS,), (STEPS, nz), (STEPS, nz), (STEPS, nz), (STEPS, nz),
        (STEPS, nz), (STEPS, nz), (STEPS, 2), (STEPS, 2), (STEPS, ny), (STEPS, ny), (STEPS, ny), (STEPS, ny),
        (STEPS, ng), (STEPS, ng), (STEPS, nz), (STEPS, nz),
    ]
    buffers = [
        (ny, qb, d), (ny, dr + 8, qb), (ny, dr + 8, qb), (ny, slots, qb),
        (STEPS, ny, d + 8, qb), (STEPS, nb, d + 8, qb),
        (STEPS, nz, dr, hq + 128), (STEPS, nz, dr, hq + 128), (STEPS, 2, nz, dr, hq + 128),
        (STEPS, 2, slots, d), (STEPS, 2, slots, d), (STEPS, 8, slots), (STEPS, 8, slots),
        (STEPS, ny, 2, slots, d), (STEPS, ny, 8, slots),
        (STEPS, 8, 128), (STEPS, ng, 8, 128), (STEPS, 8, 128), (STEPS, nz, 8, 128),
        (slots, d), (slots, d),
    ]
    vmem = pl.BlockSpec(memory_space=pltpu.VMEM)
    return pl.pallas_call(
        functools.partial(kernel, nz, ny, nx),
        out_shape=tuple(jax.ShapeDtypeStruct(x.shape, F32) for x in (compact_keys, compact_values, slot_bias)),
        in_specs=[vmem] * 6 + [pl.BlockSpec(memory_space=pltpu.SMEM)],
        out_specs=(vmem, vmem, vmem),
        scratch_shapes=[pltpu.VMEM(shape, F32) for shape in buffers]
        + [pltpu.SemaphoreType.DMA(shape) for shape in sems],
        compiler_params=pltpu.CompilerParams(collective_id=0, has_side_effects=True),
    )(queries, compact_keys, compact_values, slot_bias, targets, positions, assignment)


def solution(mesh):
    nz, ny, nx = mesh.shape["page"] // 2, mesh.shape["query"] // 2, mesh.shape["head"]
    placed = (
        P("head", "query", None),
        P("head", "page", None),
        P("head", "page", None),
        P("head", "page"),
        P("head", "query", None),
        P("head", "query"),
        P(),
    )
    return jax.shard_map(
        functools.partial(per_device, nz, ny, nx),
        mesh=mesh,
        in_specs=placed,
        out_specs=(P("head", "page", None), P("head", "page", None), P("head", "page")),
        check_vma=False,
    )
```

```python
import functools
import math

import jax
import jax.numpy as jnp
from jax import lax
from jax.experimental import pallas as pl
from jax.experimental.pallas import tpu as pltpu
from jax.sharding import PartitionSpec as P

STEPS = 2
PAGE_SHIFT = 15
MASKED = -1e30
EPSILON = 1e-06
RATE_KEYS = 0.05
RATE_VALUES = 0.05
RATE_BIAS = 0.2
HIGHEST = lax.Precision.HIGHEST
MESH = pl.DeviceIdType.MESH
F32 = jnp.float32


def dot(a, b, ca, cb):
    return lax.dot_general(
        a, b, (((ca,), (cb,)), ((), ())), precision=HIGHEST, preferred_element_type=F32
    )


def far_first(n):
    return sorted(range(1, n), key=lambda i: (-min(i, n - i), i))


def kernel(
    nz, ny, nx, q_hbm, k_hbm, v_hbm, b_in, t_hbm, pos_in, page_in, k_out, v_out, b_out,
    q_in, k_in, v_in, t_in, qg, tq, tt, tp, pgs, pg, st_s, po, pin, zs, zr, rs, rt, lse,
    gl, gr, gbl, gbr, og, ogb, s1s, s1, s2s, s2, kc, vc,
    in_sem, q_ss, q_rs, t_ss, t_rs, g_ss, g_rs, c_ss, c_rs, z_ss, z_rs, a_ss, a_rs, f_ss, f_rs, l_ss, l_rs,
    p_ss, p_rs, h_ss, h_rs, o_ss, o_rs, ob_ss, ob_rs, s1_ss, s1_rs, s2_ss, s2_rs,
):
    qb, d = q_in.shape[1:]
    slots = k_in.shape[1]
    nb = ny // 2
    hq = nb * qb
    dr = d // nz
    kr = hq // 128
    ng = ny * nx * 4
    hs = slots // 2
    scale = 1.0 / math.sqrt(d)
    slot_total = ny * nx * slots * nz * 2
    entry_count = slot_total * d

    page = lax.axis_index("page")
    z, core = page // 2, lax.rem(page, 2)
    g = lax.axis_index("query")
    y, xh = g // 2, lax.rem(g, 2)
    xl = lax.axis_index("head")
    gi = (g * nx + xl) * 2 + core
    y_half, y_in = y // nb, lax.rem(y, nb)
    z_rows = pl.ds(pl.multiple_of(z * dr, dr), dr)

    def at_z(i):
        other = lax.rem(z + i, nz)
        return other, {"page": other * 2 + core}

    def at_y(i):
        other = lax.rem(y + i, ny)
        return other, {"query": other * 2 + xh}

    def at_g(i):
        other = lax.rem(gi + i, ng)
        oc = lax.rem(other, 2)
        ox = lax.rem(other // 2, nx)
        return other, {"page": z * 2 + oc, "query": other // (2 * nx), "head": ox}

    def at_head(j, i):
        other = lax.rem(z + i, nz)
        return other, {"page": other * 2 + y_half, "query": (core * nb + j) * 2 + xh}

    other_core = {"page": z * 2 + 1 - core}
    pair = {"query": y * 2 + 1 - xh}

    barrier = pltpu.get_barrier_semaphore()
    for i in range(1, nz):
        for j in range(nb):
            pl.semaphore_signal(barrier, inc=1, device_id=at_head(j, i)[1], device_id_type=MESH)
        pl.semaphore_signal(barrier, inc=1, device_id=at_z(i)[1], device_id_type=MESH)
    for i in range(1, ng):
        pl.semaphore_signal(barrier, inc=1, device_id=at_g(i)[1], device_id_type=MESH)

    loads = [
        pltpu.make_async_copy(src, dst, in_sem.at[n])
        for n, (src, dst) in enumerate(((q_hbm, q_in), (k_hbm, k_in), (v_hbm, v_in), (t_hbm, t_in)))
    ]
    for load in loads:
        load.start()

    pending = []

    def send(src, dst, ss, rs_, dev, when=None):
        copy = pltpu.make_async_remote_copy(
            src_ref=src, dst_ref=dst, send_sem=ss, recv_sem=rs_, device_id=dev, device_id_type=MESH
        )
        if when is None:
            copy.start()
        else:
            pl.when(when)(copy.start)
        pending.append((copy, when))

    def arrive(dst, ss, rs_, dev, when=None):
        copy = pltpu.make_async_remote_copy(
            src_ref=dst, dst_ref=dst, send_sem=ss, recv_sem=rs_, device_id=dev, device_id_type=MESH
        )
        if when is None:
            copy.wait_recv()
        else:
            pl.when(when)(copy.wait_recv)

    def column(row):
        return jnp.transpose(jnp.broadcast_to(row, (128, slots)))[:, :1]

    def stack_rows(rows, height, width):
        at = lax.broadcasted_iota(jnp.int32, (height, width), 0)
        tile = jnp.zeros((height, width), F32)
        for r, row in enumerate(rows):
            tile = jnp.where(at == r, jnp.broadcast_to(row, (height, width)), tile)
        return tile

    def forward(step, blk, scores, seen, values):
        top = jnp.max(scores, axis=0, keepdims=True)
        weights = jnp.where(seen, jnp.exp(scores - top), 0.0)
        po[step, blk, :d, :] = dot(values, weights, 0, 0)
        total = jnp.sum(weights, axis=0, keepdims=True)
        po[step, blk, d:, :] = stack_rows([top, total], 8, qb)

    my_page = page_in[page].astype(F32)
    pages = (pos_in[...] >> PAGE_SHIFT).astype(F32)
    for h in range(ny):
        pgs[h] = pages[h : h + 1]
    row_of = lax.broadcasted_iota(jnp.int32, (ny, slots), 0)
    bias_row = jnp.sum(jnp.where(row_of == y, b_in[...], 0.0), axis=0, keepdims=True)
    for load in loads:
        load.wait()
    for h in range(ny):
        seen = my_page <= pages[h : h + 1]
        scores = dot(k_in[h], q_in[h], 1, 1) * scale + column(b_in[h : h + 1])
        forward(0, h, jnp.where(seen, scores, MASKED), seen, v_in[h])

    pl.semaphore_wait(barrier, (nz - 1) * (nb + 1) + ng - 1)

    def share_core(step):
        give = pl.ds((1 - core) * nb, nb)
        send(po.at[step, give], pin.at[step], c_ss.at[step], c_rs.at[step], other_core)

    share_core(0)
    for i in range(1, ny):
        other, dev = at_y(i)
        send(q_in.at[other], qg.at[y], q_ss.at[other], q_rs.at[y], dev)
        send(t_in.at[other], tq.at[y], t_ss.at[other], t_rs.at[y], dev)
        send(pgs.at[other], pg.at[y], g_ss.at[other], g_rs.at[y], dev)
    pick = (
        lax.broadcasted_iota(jnp.int32, (dr, d), 1)
        == lax.broadcasted_iota(jnp.int32, (dr, d), 0) + z * dr
    ).astype(F32)
    for j in range(nb):
        tp[j] = dot(pick, t_in[core * nb + j], 1, 1)
    qg[y] = q_in[y]
    tq[y] = t_in[y]
    pg[y] = pgs[y]
    kc[...] = k_in[y]
    vc[...] = v_in[y]

    rates = []
    for step in range(STEPS):
        keys, values = kc[...], vc[...]
        bias_col = column(bias_row)
        if step:
            for blk in range(ny):
                seen = my_page <= pg[blk]
                scores = jnp.where(seen, dot(keys, qg[blk], 1, 1) * scale + bias_col, MASKED)
                st_s[blk] = scores
                forward(step, blk, scores, seen, values)
            share_core(step)

        arrive(pin.at[step], c_ss.at[step], c_rs.at[step], other_core)
        tops, totals = [], []
        for j in range(nb):
            mine, theirs = po[step, core * nb + j], pin[step, j]
            m0, m1 = mine[d : d + 1], theirs[d : d + 1]
            top = jnp.maximum(m0, m1)
            f0, f1 = jnp.exp(m0 - top), jnp.exp(m1 - top)
            zs[step, :, :, j * qb : (j + 1) * qb] = (mine[:d] * f0 + theirs[:d] * f1).reshape(nz, dr, qb)
            total = mine[d + 1 : d + 2] * f0 + theirs[d + 1 : d + 2] * f1
            for a in range(0, qb, 128):
                tops.append(top[:, a : a + 128])
                totals.append(total[:, a : a + 128])
        tile = stack_rows(tops + totals, dr, 128)
        zs[step, :, :, hq:] = jnp.broadcast_to(tile[None], (nz, dr, 128))

        for i in far_first(nz):
            other, dev = at_z(i)
            send(zs.at[step, other], zr.at[step, z], z_ss.at[step, other], z_rs.at[step, z], dev)
        zr[step, z] = zs[step, z]
        for i in range(1, nz):
            other, dev = at_z(i)
            arrive(zr.at[step, other], z_ss.at[step, other], z_rs.at[step, other], dev)
        for r in range(kr):
            lanes = slice(r * 128, (r + 1) * 128)
            m_all = zr[step, :, r, hq:]
            l_all = zr[step, :, kr + r, hq:]
            top = jnp.max(m_all, axis=0, keepdims=True)
            f_all = jnp.exp(m_all - top)
            total = jnp.sum(f_all * l_all, axis=0, keepdims=True)
            output = jnp.sum(zr[step, :, :, lanes] * f_all[:, None, :], axis=0) / total
            j, off = (r * 128) // qb, (r * 128) % qb
            blk = core * nb + j
            target = tp[j, :, off : off + 128] if step == 0 else tt[blk, z_rows, off : off + 128]
            rs[step, j, :, off : off + 128] = output - target
            lse[step, ny if step == 0 else blk, j, :, off : off + 128] = top + jnp.log(total)

        for i in far_first(nz):
            for j in range(nb):
                blk = y if step == 0 else core * nb + j
                other, dev = at_head(j, i) if step == 0 else at_z(i)
                slot = y_in if step == 0 else j
                send(rs.at[step, j], rt.at[step, blk, z_rows], a_ss.at[step, j, other], a_rs.at[step, slot, z], dev)
        if step == 0:
            for j in range(nb):
                head = core * nb + j
                dev = at_head(j, 0)[1]
                away = head != y
                send(rs.at[0, j], rt.at[0, y, z_rows], a_ss.at[0, j, z], a_rs.at[0, y_in, z], dev, away)
                for c in range(2):
                    dev = {"page": z * 2 + c, "query": head * 2 + xh}
                    away = jnp.logical_or(head != y, core != c)
                    send(lse.at[0, ny, j], lse.at[0, y, 0], l_ss.at[0, j, c], l_rs.at[0, y], dev, away)

                @pl.when(head == y)
                def _(j=j):
                    rt[0, y, z_rows, :] = rs[0, j]
                    lse[0, y, 0] = lse[0, ny, j]

            for i in range(ny):
                blk, dev = at_y(i)
                if i:
                    arrive(qg.at[blk], q_ss.at[blk], q_rs.at[blk], dev)
                    arrive(tq.at[blk], t_ss.at[blk], t_rs.at[blk], dev)
                    arrive(pg.at[blk], g_ss.at[blk], g_rs.at[blk], dev)
                scores = dot(keys, qg[blk], 1, 1) * scale + bias_col
                st_s[blk] = jnp.where(my_page <= pg[blk], scores, MASKED)
                tt[blk] = jnp.transpose(tq[blk])
        else:
            for j in range(nb):
                rt[step, core * nb + j, z_rows, :] = rs[step, j]
                mine = lse.at[step, core * nb + j, j]
                send(mine, lse.at[step, core * nb + j, j], l_ss.at[step, j, 0], l_rs.at[step, core * nb + j], other_core)
        for i in [0] + far_first(nz)[::-1]:
            other, dev = at_z(i)
            rows = pl.ds(pl.multiple_of(other * dr, dr), dr)
            for j in range(nb):
                blk = core * nb + j
                when = None
                if step == 0:
                    dev = {"page": other * 2 + y_half, "query": blk * 2 + xh}
                    if i == 0:
                        when = blk != y
                elif i == 0:
                    continue
                arrive(rt.at[step, blk, rows], a_ss.at[step, j, other], a_rs.at[step, j, other], dev, when)
            there = rt.at[step, pl.ds(core * nb, nb), rows]
            send(there, there, f_ss.at[step, other], f_rs.at[step, other], other_core)

        if step == 0:
            for blk in range(ny):
                when = jnp.logical_or(blk != y, y_half != core)
                dev = {"page": z * 2 + y_half, "query": blk * 2 + xh}
                arrive(lse.at[0, blk, 0], l_ss.at[0, 0, 0], l_rs.at[0, blk], dev, when)
        grad_keys = jnp.zeros((slots, d), F32)
        grad_values = jnp.zeros((slots, d), F32)
        grad_bias = jnp.zeros((8, slots), F32)
        for late in range(2):
            half = core if late == 0 else 1 - core
            if late:
                for i in range(nz):
                    other = lax.rem(z + i, nz)
                    rows = pl.ds(pl.multiple_of(other * dr, dr), dr)
                    there = rt.at[step, pl.ds(half * nb, nb), rows]
                    arrive(there, f_ss.at[step, other], f_rs.at[step, other], other_core)
                if step:
                    for j in range(nb):
                        blk = half * nb + j
                        arrive(lse.at[step, blk, j], l_ss.at[step, j, 0], l_rs.at[step, blk], other_core)
            for j in range(nb):
                blk = half * nb + j
                residual = rt[step, blk]
                delta = jnp.sum(residual * (residual + tt[blk]), axis=0, keepdims=True)
                attention = jnp.exp(st_s[blk] - lse[step, blk, j if step else 0])
                grad_values += dot(attention, residual, 1, 1)
                grad_scores = attention * (dot(values, residual, 1, 0) - delta)
                grad_keys += dot(grad_scores, qg[blk], 1, 0)
                grad_bias += dot(jnp.ones((8, qb), F32), grad_scores, 1, 1)
        for s in range(2):
            gl[step, s, 0] = grad_keys[s * hs : (s + 1) * hs] * scale
            gl[step, s, 1] = grad_values[s * hs : (s + 1) * hs]
            gbl[step, s] = grad_bias[:, s * hs : (s + 1) * hs]
        send(gl.at[step, 1 - xh], gr.at[step], p_ss.at[step, 0], p_rs.at[step, 0], pair)
        send(gbl.at[step, 1 - xh], gbr.at[step], p_ss.at[step, 1], p_rs.at[step, 1], pair)
        arrive(gr.at[step], p_ss.at[step, 0], p_rs.at[step, 0], pair)
        arrive(gbr.at[step], p_ss.at[step, 1], p_rs.at[step, 1], pair)
        grad_keys = gl[step, xh, 0] + gr[step, 0]
        grad_values = gl[step, xh, 1] + gr[step, 1]
        grad_bias = gbl[step, xh] + gbr[step]
        squares = jnp.sum(grad_bias[:1] * grad_bias[:1], axis=1, keepdims=True) / 128
        s1s[step] = stack_rows(
            [
                jnp.sum(grad_keys * grad_keys, axis=0, keepdims=True),
                jnp.sum(grad_values * grad_values, axis=0, keepdims=True),
                jnp.broadcast_to(squares, (1, 128)),
            ],
            8,
            128,
        )
        for i in range(1, ng):
            other, dev = at_g(i)
            send(s1s.at[step], s1.at[step, gi], s1_ss.at[step, other], s1_rs.at[step, gi], dev)
        s1[step, gi] = s1s[step]
        og[step, y, xh, 0] = grad_keys
        og[step, y, xh, 1] = grad_values
        ogb[step, y, xh] = grad_bias
        mine, mine_b = og.at[step, y, xh], ogb.at[step, y, xh]
        send(mine, mine, h_ss.at[step, 0], h_rs.at[step, 0], pair)
        send(mine_b, mine_b, h_ss.at[step, 1], h_rs.at[step, 1], pair)
        for i in range(1, ny):
            other, dev = at_y(i)
            send(mine, mine, o_ss.at[step, other, xh], o_rs.at[step, y, xh], dev)
            send(mine_b, mine_b, ob_ss.at[step, other, xh], ob_rs.at[step, y, xh], dev)
        for i in range(1, ng):
            other, dev = at_g(i)
            arrive(s1.at[step, other], s1_ss.at[step, other], s1_rs.at[step, other], dev)
        s2s[step] = jnp.sum(s1[step], axis=0)
        for i in far_first(nz):
            other, dev = at_z(i)
            send(s2s.at[step], s2.at[step, z], s2_ss.at[step, other], s2_rs.at[step, z], dev)
        s2[step, z] = s2s[step]
        theirs, theirs_b = og.at[step, y, 1 - xh], ogb.at[step, y, 1 - xh]
        arrive(theirs, h_ss.at[step, 0], h_rs.at[step, 0], pair)
        arrive(theirs_b, h_ss.at[step, 1], h_rs.at[step, 1], pair)
        for i in range(1, ny):
            other, dev = at_y(i)
            send(theirs, theirs, o_ss.at[step, other, 1 - xh], o_rs.at[step, y, 1 - xh], dev)
            send(theirs_b, theirs_b, ob_ss.at[step, other, 1 - xh], ob_rs.at[step, y, 1 - xh], dev)
        for i in range(1, nz):
            other, dev = at_z(i)
            arrive(s2.at[step, other], s2_ss.at[step, other], s2_rs.at[step, other], dev)
        sums = jnp.sum(jnp.sum(s2[step], axis=0), axis=1, keepdims=True)
        rate_keys = RATE_KEYS / jnp.sqrt(sums[0:1] / entry_count + EPSILON)
        rate_values = RATE_VALUES / jnp.sqrt(sums[1:2] / entry_count + EPSILON)
        rate_bias = RATE_BIAS / jnp.sqrt(sums[2:3] / slot_total + EPSILON)
        rates.append((rate_keys, rate_values, rate_bias))
        if step < STEPS - 1:
            for s in range(2):
                part = slice(s * hs, (s + 1) * hs)
                kc[part] = keys[part] - rate_keys * og[step, y, s, 0]
                vc[part] = values[part] - rate_values * og[step, y, s, 1]
            whole = jnp.concatenate([ogb[step, y, 0, :1], ogb[step, y, 1, :1]], axis=1)
            bias_row = bias_row - rate_bias * whole

    for step in range(STEPS):
        for i in range(1, ny):
            other, dev = at_y(i)
            for s in (xh, 1 - xh):
                arrive(og.at[step, other, s], o_ss.at[step, other, s], o_rs.at[step, other, s], dev)
                arrive(ogb.at[step, other, s], ob_ss.at[step, other, s], ob_rs.at[step, other, s], dev)
    for h in range(ny):
        for s in range(2):
            part = slice(s * hs, (s + 1) * hs)
            new_keys, new_values, new_bias = k_in[h, part], v_in[h, part], b_in[h : h + 1, part]
            for step in range(STEPS):
                rate_keys, rate_values, rate_bias = rates[step]
                new_keys = new_keys - rate_keys * og[step, h, s, 0]
                new_values = new_values - rate_values * og[step, h, s, 1]
                new_bias = new_bias - rate_bias * ogb[step, h, s, :1]
            k_out[h, part] = new_keys
            v_out[h, part] = new_values
            b_out[h : h + 1, part] = new_bias
    for copy, when in pending:
        if when is None:
            copy.wait_send()
        else:
            pl.when(when)(copy.wait_send)


def per_device(nz, ny, nx, queries, compact_keys, compact_values, slot_bias, targets, positions, assignment):
    qb, d = queries.shape[1:]
    slots = compact_keys.shape[1]
    nb = ny // 2
    hq, dr, ng, hs = nb * qb, d // nz, ny * nx * 4, slots // 2
    sems = [(4,)]
    for shape in (
        (ny,), (ny,), (ny,), (STEPS,), (STEPS, nz), (STEPS, nb, nz), (STEPS, nz), (STEPS, nb, 2), (STEPS, 2),
        (STEPS, 2), (STEPS, ny, 2), (STEPS, ny, 2), (STEPS, ng), (STEPS, nz),
    ):
        sems += [shape, shape]
    sems[16] = (STEPS, ny)
    buffers = [
        (ny, qb, d), (ny, slots, d), (ny, slots, d), (ny, qb, d),
        (ny, qb, d), (ny, qb, d), (ny, d, qb), (nb, dr, qb), (ny, 1, qb), (ny, 1, qb), (ny, slots, qb),
        (STEPS, ny, d + 8, qb), (STEPS, nb, d + 8, qb),
        (STEPS, nz, dr, hq + 128), (STEPS, nz, dr, hq + 128),
        (STEPS, nb, dr, qb), (STEPS, ny, d, qb), (STEPS, ny + 1, nb, 1, qb),
        (STEPS, 2, 2, hs, d), (STEPS, 2, hs, d), (STEPS, 2, 8, hs), (STEPS, 8, hs),
        (STEPS, ny, 2, 2, hs, d), (STEPS, ny, 2, 8, hs),
        (STEPS, 8, 128), (STEPS, ng, 8, 128), (STEPS, 8, 128), (STEPS, nz, 8, 128),
        (slots, d), (slots, d),
    ]
    vmem, hbm = pl.BlockSpec(memory_space=pltpu.VMEM), pl.BlockSpec(memory_space=pl.ANY)
    return pl.pallas_call(
        functools.partial(kernel, nz, ny, nx),
        out_shape=tuple(jax.ShapeDtypeStruct(x.shape, F32) for x in (compact_keys, compact_values, slot_bias)),
        in_specs=[hbm, hbm, hbm, vmem, hbm, vmem, pl.BlockSpec(memory_space=pltpu.SMEM)],
        out_specs=(vmem, vmem, vmem),
        scratch_shapes=[pltpu.VMEM(shape, F32) for shape in buffers]
        + [pltpu.SemaphoreType.DMA(shape) for shape in sems],
        compiler_params=pltpu.CompilerParams(collective_id=0, has_side_effects=True),
    )(queries, compact_keys, compact_values, slot_bias, targets, positions, assignment)


def solution(mesh):
    nz, ny, nx = mesh.shape["page"] // 2, mesh.shape["query"] // 2, mesh.shape["head"]
    placed = (
        P("head", "query", None),
        P("head", "page", None),
        P("head", "page", None),
        P("head", "page"),
        P("head", "query", None),
        P("head", "query"),
        P(),
    )
    return jax.shard_map(
        functools.partial(per_device, nz, ny, nx),
        mesh=mesh,
        in_specs=placed,
        out_specs=(P("head", "page", None), P("head", "page", None), P("head", "page")),
        check_vma=False,
    )
```

```python
import functools
import math

import jax
import jax.numpy as jnp
from jax import lax
from jax.experimental import pallas as pl
from jax.experimental.pallas import tpu as pltpu
from jax.sharding import PartitionSpec as P

STEPS = 2
PAGE_SHIFT = 15
MASKED = -1e30
EPSILON = 1e-06
RATE_KEYS = 0.05
RATE_VALUES = 0.05
RATE_BIAS = 0.2
HIGHEST = lax.Precision.HIGHEST
HIGH = lax.Precision.HIGH
MESH = pl.DeviceIdType.MESH
F32 = jnp.float32


def dot(a, b, ca, cb, precision=HIGH):
    return lax.dot_general(
        a, b, (((ca,), (cb,)), ((), ())), precision=precision, preferred_element_type=F32
    )


def far_first(n):
    return sorted(range(1, n), key=lambda i: (-min(i, n - i), i))


def kernel(
    nz, ny, nx, q_hbm, k_hbm, v_hbm, b_in, t_hbm, pos_in, page_in, k_out, v_out, b_out,
    q_in, k_in, v_in, t_in, qg, tq, tt, tp, pgs, pg, st_s, po, pin, zs, zr, zt, ztr, rs, rt, lse,
    gl, gr, gbl, gbr, og, ogb, s1s, s1, s2s, s2, kc, vc,
    in_sem, q_ss, q_rs, t_ss, t_rs, g_ss, g_rs, c_ss, c_rs, z_ss, z_rs, a_ss, a_rs, f_ss, f_rs, l_ss, l_rs,
    p_ss, p_rs, h_ss, h_rs, o_ss, o_rs, ob_ss, ob_rs, s1_ss, s1_rs, s2_ss, s2_rs, y_ss, y_rs,
):
    qb, d = q_in.shape[1:]
    slots = k_in.shape[1]
    nb = ny // 2
    hq = nb * qb
    dr = d // nz
    kr = hq // 128
    ng = ny * nx * 4
    hs = slots // 2
    scale = 1.0 / math.sqrt(d)
    slot_total = ny * nx * slots * nz * 2
    entry_count = slot_total * d

    page = lax.axis_index("page")
    z, core = page // 2, lax.rem(page, 2)
    g = lax.axis_index("query")
    y, xh = g // 2, lax.rem(g, 2)
    xl = lax.axis_index("head")
    gi = (g * nx + xl) * 2 + core
    y_half, y_in = y // nb, lax.rem(y, nb)
    z_rows = pl.ds(pl.multiple_of(z * dr, dr), dr)

    def at_z(i):
        other = lax.rem(z + i, nz)
        return other, {"page": other * 2 + core}

    def at_y(i):
        other = lax.rem(y + i, ny)
        return other, {"query": other * 2 + xh}

    def at_g(i):
        other = lax.rem(gi + i, ng)
        oc = lax.rem(other, 2)
        ox = lax.rem(other // 2, nx)
        return other, {"page": z * 2 + oc, "query": other // (2 * nx), "head": ox}

    def at_head(j, i):
        other = lax.rem(z + i, nz)
        return other, {"page": other * 2 + y_half, "query": (core * nb + j) * 2 + xh}

    other_core = {"page": z * 2 + 1 - core}
    pair = {"query": y * 2 + 1 - xh}

    loads = [
        pltpu.make_async_copy(src, dst, in_sem.at[n])
        for n, (src, dst) in enumerate(((q_hbm, q_in), (k_hbm, k_in), (v_hbm, v_in), (t_hbm, t_in)))
    ]
    for load in loads:
        load.start()

    barrier = pltpu.get_barrier_semaphore()
    for i in range(1, nz):
        for j in range(nb):
            pl.semaphore_signal(barrier, inc=1, device_id=at_head(j, i)[1], device_id_type=MESH)
        pl.semaphore_signal(barrier, inc=1, device_id=at_z(i)[1], device_id_type=MESH)
    for i in range(1, ng):
        pl.semaphore_signal(barrier, inc=1, device_id=at_g(i)[1], device_id_type=MESH)

    pending = []

    def send(src, dst, ss, rs_, dev, when=None):
        copy = pltpu.make_async_remote_copy(
            src_ref=src, dst_ref=dst, send_sem=ss, recv_sem=rs_, device_id=dev, device_id_type=MESH
        )
        if when is None:
            copy.start()
        else:
            pl.when(when)(copy.start)
        pending.append((copy, when))

    def arrive(dst, ss, rs_, dev, when=None):
        copy = pltpu.make_async_remote_copy(
            src_ref=dst, dst_ref=dst, send_sem=ss, recv_sem=rs_, device_id=dev, device_id_type=MESH
        )
        if when is None:
            copy.wait_recv()
        else:
            pl.when(when)(copy.wait_recv)

    def column(row):
        return jnp.transpose(jnp.broadcast_to(row, (128, slots)))[:, :1]

    def stack_rows(rows, height, width):
        at = lax.broadcasted_iota(jnp.int32, (height, width), 0)
        tile = jnp.zeros((height, width), F32)
        for r, row in enumerate(rows):
            tile = jnp.where(at == r, jnp.broadcast_to(row, (height, width)), tile)
        return tile

    def forward(step, blk, scores, seen, values):
        top = jnp.max(scores, axis=0, keepdims=True)
        weights = jnp.where(seen, jnp.exp(scores - top), 0.0)
        po[step, blk, :d, :] = dot(values, weights, 0, 0)
        total = jnp.sum(weights, axis=0, keepdims=True)
        po[step, blk, d:, :] = stack_rows([top, total], 8, qb)

    def share_core(step, j):
        c_ss_, c_rs_ = c_ss.at[step, j], c_rs.at[step, j]
        send(po.at[step, (1 - core) * nb + j], pin.at[step, j], c_ss_, c_rs_, other_core)

    my_page = page_in[page].astype(F32)
    pages = (pos_in[...] >> PAGE_SHIFT).astype(F32)
    for h in range(ny):
        pgs[h] = pages[h : h + 1]
    row_of = lax.broadcasted_iota(jnp.int32, (ny, slots), 0)

    def bias_of(h):
        return jnp.sum(jnp.where(row_of == h, b_in[...], 0.0), axis=0, keepdims=True)

    def first_forward(h):
        seen = my_page <= pgs[h]
        scores = dot(k_in[h], q_in[h], 1, 1, HIGHEST) * scale + column(bias_of(h))
        forward(0, h, jnp.where(seen, scores, MASKED), seen, v_in[h])

    for load in loads:
        load.wait()
    for j in range(nb):
        first_forward((1 - core) * nb + j)

    pl.semaphore_wait(barrier, (nz - 1) * (nb + 1) + ng - 1)

    for j in range(nb):
        share_core(0, j)
    for i in range(1, ny):
        other, dev = at_y(i)
        send(q_in.at[other], qg.at[y], q_ss.at[other], q_rs.at[y], dev)
        send(t_in.at[other], tq.at[y], t_ss.at[other], t_rs.at[y], dev)
        send(pgs.at[other], pg.at[y], g_ss.at[other], g_rs.at[y], dev)
    for j in range(nb):
        first_forward(core * nb + j)
    bias_row = bias_of(y)

    rates = []
    for step in range(STEPS):
        if step:
            keys, values = kc[...], vc[...]
            bias_col = column(bias_row)
            for n in range(ny):
                blk = (1 - core) * nb + n if n < nb else core * nb + n - nb
                seen = my_page <= pg[blk]
                scores = jnp.where(seen, dot(keys, qg[blk], 1, 1, HIGHEST) * scale + bias_col, MASKED)
                st_s[blk] = scores
                forward(step, blk, scores, seen, values)
                if n < nb:
                    share_core(step, n)

        stats = []
        for j in range(nb):
            arrive(pin.at[step, j], c_ss.at[step, j], c_rs.at[step, j], other_core)
            mine, theirs = po[step, core * nb + j], pin[step, j]
            m0, m1 = mine[d : d + 1], theirs[d : d + 1]
            top = jnp.maximum(m0, m1)
            f0, f1 = jnp.exp(m0 - top), jnp.exp(m1 - top)
            total = mine[d + 1 : d + 2] * f0 + theirs[d + 1 : d + 2] * f1
            some = total > 0.0
            inverse = jnp.where(some, 1.0 / jnp.where(some, total, 1.0), 0.0)
            merged = mine[:d] * (f0 * inverse) + theirs[:d] * (f1 * inverse)
            zs[step, :, :, j * qb : (j + 1) * qb] = merged.reshape(nz, dr, qb)
            chip = jnp.where(some, top + jnp.log(jnp.where(some, total, 1.0)), MASKED)
            stats += [chip[:, a : a + 128] for a in range(0, qb, 128)]
        tile = stack_rows(stats, kr, 128)
        zt[step] = tile

        for i in far_first(nz):
            other, dev = at_z(i)
            send(zt.at[step], ztr.at[step, z], y_ss.at[step, other], y_rs.at[step, z], dev)
            send(zs.at[step, other], zr.at[step, z], z_ss.at[step, other], z_rs.at[step, z], dev)
        zr[step, z] = zs[step, z]
        ztr[step, z] = tile
        if step == 0:
            pick = (
                lax.broadcasted_iota(jnp.int32, (dr, d), 1)
                == lax.broadcasted_iota(jnp.int32, (dr, d), 0) + z * dr
            ).astype(F32)
            for j in range(nb):
                tp[j] = dot(pick, t_in[core * nb + j], 1, 1, HIGHEST)
            qg[y] = q_in[y]
            tq[y] = t_in[y]
            pg[y] = pgs[y]
            kc[...] = k_in[y]
            vc[...] = v_in[y]
            keys, values = kc[...], vc[...]
            bias_col = column(bias_row)
        for i in far_first(nz):
            other, dev = at_z(i)
            arrive(ztr.at[step, other], y_ss.at[step, other], y_rs.at[step, other], dev)
            arrive(zr.at[step, other], z_ss.at[step, other], z_rs.at[step, other], dev)
        for r in range(kr):
            lanes = slice(r * 128, (r + 1) * 128)
            l_all = ztr[step, :, r, :]
            top = jnp.max(l_all, axis=0, keepdims=True)
            f_all = jnp.exp(l_all - top)
            total = jnp.sum(f_all, axis=0, keepdims=True)
            output = jnp.sum(zr[step, :, :, lanes] * f_all[:, None, :], axis=0) / total
            j, off = (r * 128) // qb, (r * 128) % qb
            blk = core * nb + j
            target = tp[j, :, off : off + 128] if step == 0 else tt[blk, z_rows, off : off + 128]
            rs[step, j, :, off : off + 128] = output - target
            lse[step, ny if step == 0 else blk, j, :, off : off + 128] = top + jnp.log(total)

        if step == 0:
            for j in range(nb):
                head = core * nb + j
                dev = at_head(j, 0)[1]
                away = head != y
                send(rs.at[0, j], rt.at[0, y, z_rows], a_ss.at[0, j, z], a_rs.at[0, y_in, z], dev, away)
                for c in range(2):
                    dev = {"page": z * 2 + c, "query": head * 2 + xh}
                    away = jnp.logical_or(head != y, core != c)
                    send(lse.at[0, ny, j], lse.at[0, y, 0], l_ss.at[0, j, c], l_rs.at[0, y], dev, away)

                @pl.when(head == y)
                def _(j=j):
                    rt[0, y, z_rows, :] = rs[0, j]
                    lse[0, y, 0] = lse[0, ny, j]

        for i in far_first(nz):
            for j in range(nb):
                blk = y if step == 0 else core * nb + j
                other, dev = at_head(j, i) if step == 0 else at_z(i)
                slot = y_in if step == 0 else j
                send(rs.at[step, j], rt.at[step, blk, z_rows], a_ss.at[step, j, other], a_rs.at[step, slot, z], dev)
        if step == 0:
            for i in range(ny):
                blk, dev = at_y(i)
                if i:
                    arrive(qg.at[blk], q_ss.at[blk], q_rs.at[blk], dev)
                    arrive(tq.at[blk], t_ss.at[blk], t_rs.at[blk], dev)
                    arrive(pg.at[blk], g_ss.at[blk], g_rs.at[blk], dev)
                scores = dot(keys, qg[blk], 1, 1, HIGHEST) * scale + bias_col
                st_s[blk] = jnp.where(my_page <= pg[blk], scores, MASKED)
                tt[blk] = jnp.transpose(tq[blk])
        else:
            for j in range(nb):
                rt[step, core * nb + j, z_rows, :] = rs[step, j]
                mine = lse.at[step, core * nb + j, j]
                send(mine, lse.at[step, core * nb + j, j], l_ss.at[step, j, 0], l_rs.at[step, core * nb + j], other_core)
        for i in [0] + far_first(nz):
            other, dev = at_z(i)
            rows = pl.ds(pl.multiple_of(other * dr, dr), dr)
            for j in range(nb):
                blk = core * nb + j
                when = None
                if step == 0:
                    dev = {"page": other * 2 + y_half, "query": blk * 2 + xh}
                    if i == 0:
                        when = blk != y
                elif i == 0:
                    continue
                arrive(rt.at[step, blk, rows], a_ss.at[step, j, other], a_rs.at[step, j, other], dev, when)
            there = rt.at[step, pl.ds(core * nb, nb), rows]
            send(there, there, f_ss.at[step, other], f_rs.at[step, other], other_core)

        if step == 0:
            for blk in range(ny):
                when = jnp.logical_or(blk != y, y_half != core)
                dev = {"page": z * 2 + y_half, "query": blk * 2 + xh}
                arrive(lse.at[0, blk, 0], l_ss.at[0, 0, 0], l_rs.at[0, blk], dev, when)
        grad_keys = jnp.zeros((slots, d), F32)
        grad_values = jnp.zeros((slots, d), F32)
        grad_bias = jnp.zeros((8, slots), F32)
        for late in range(2):
            half = core if late == 0 else 1 - core
            if late:
                for i in [0] + far_first(nz):
                    other = lax.rem(z + i, nz)
                    rows = pl.ds(pl.multiple_of(other * dr, dr), dr)
                    there = rt.at[step, pl.ds(half * nb, nb), rows]
                    arrive(there, f_ss.at[step, other], f_rs.at[step, other], other_core)
                if step:
                    for j in range(nb):
                        blk = half * nb + j
                        arrive(lse.at[step, blk, j], l_ss.at[step, j, 0], l_rs.at[step, blk], other_core)
            for j in range(nb):
                blk = half * nb + j
                residual = rt[step, blk]
                delta = jnp.sum(residual * (residual + tt[blk]), axis=0, keepdims=True)
                attention = jnp.exp(st_s[blk] - lse[step, blk, j if step else 0])
                grad_values += dot(attention, residual, 1, 1)
                grad_scores = attention * (dot(values, residual, 1, 0) - delta)
                grad_keys += dot(grad_scores, qg[blk], 1, 0)
                grad_bias += dot(jnp.ones((8, qb), F32), grad_scores, 1, 1)
        for s in range(2):
            gl[step, s, 0] = grad_keys[s * hs : (s + 1) * hs] * scale
            gl[step, s, 1] = grad_values[s * hs : (s + 1) * hs]
            gbl[step, s] = grad_bias[:, s * hs : (s + 1) * hs]
        send(gl.at[step, 1 - xh], gr.at[step], p_ss.at[step, 0], p_rs.at[step, 0], pair)
        send(gbl.at[step, 1 - xh], gbr.at[step], p_ss.at[step, 1], p_rs.at[step, 1], pair)
        arrive(gr.at[step], p_ss.at[step, 0], p_rs.at[step, 0], pair)
        arrive(gbr.at[step], p_ss.at[step, 1], p_rs.at[step, 1], pair)
        grad_keys = gl[step, xh, 0] + gr[step, 0]
        grad_values = gl[step, xh, 1] + gr[step, 1]
        grad_bias = gbl[step, xh] + gbr[step]
        squares = jnp.sum(grad_bias[:1] * grad_bias[:1], axis=1, keepdims=True) / 128
        s1s[step] = stack_rows(
            [
                jnp.sum(grad_keys * grad_keys, axis=0, keepdims=True),
                jnp.sum(grad_values * grad_values, axis=0, keepdims=True),
                jnp.broadcast_to(squares, (1, 128)),
            ],
            8,
            128,
        )
        for i in range(1, ng):
            other, dev = at_g(i)
            send(s1s.at[step], s1.at[step, gi], s1_ss.at[step, other], s1_rs.at[step, gi], dev)
        s1[step, gi] = s1s[step]
        og[step, y, xh, 0] = grad_keys
        og[step, y, xh, 1] = grad_values
        ogb[step, y, xh] = grad_bias
        mine, mine_b = og.at[step, y, xh], ogb.at[step, y, xh]

        def gather(step=step, mine=mine, mine_b=mine_b):
            send(mine, mine, h_ss.at[step, 0], h_rs.at[step, 0], pair)
            send(mine_b, mine_b, h_ss.at[step, 1], h_rs.at[step, 1], pair)
            for i in range(1, ny):
                other, dev = at_y(i)
                send(mine, mine, o_ss.at[step, other, xh], o_rs.at[step, y, xh], dev)
                send(mine_b, mine_b, ob_ss.at[step, other, xh], ob_rs.at[step, y, xh], dev)

        if step == STEPS - 1:
            gather()
        for i in range(1, ng):
            other, dev = at_g(i)
            arrive(s1.at[step, other], s1_ss.at[step, other], s1_rs.at[step, other], dev)
        s2s[step] = jnp.sum(s1[step], axis=0)
        for i in far_first(nz):
            other, dev = at_z(i)
            send(s2s.at[step], s2.at[step, z], s2_ss.at[step, other], s2_rs.at[step, z], dev)
        s2[step, z] = s2s[step]
        if step < STEPS - 1:
            gather()
        theirs, theirs_b = og.at[step, y, 1 - xh], ogb.at[step, y, 1 - xh]
        arrive(theirs, h_ss.at[step, 0], h_rs.at[step, 0], pair)
        arrive(theirs_b, h_ss.at[step, 1], h_rs.at[step, 1], pair)
        for i in range(1, ny):
            other, dev = at_y(i)
            send(theirs, theirs, o_ss.at[step, other, 1 - xh], o_rs.at[step, y, 1 - xh], dev)
            send(theirs_b, theirs_b, ob_ss.at[step, other, 1 - xh], ob_rs.at[step, y, 1 - xh], dev)
        for i in range(1, nz):
            other, dev = at_z(i)
            arrive(s2.at[step, other], s2_ss.at[step, other], s2_rs.at[step, other], dev)
        sums = jnp.sum(jnp.sum(s2[step], axis=0), axis=1, keepdims=True)
        rate_keys = RATE_KEYS / jnp.sqrt(sums[0:1] / entry_count + EPSILON)
        rate_values = RATE_VALUES / jnp.sqrt(sums[1:2] / entry_count + EPSILON)
        rate_bias = RATE_BIAS / jnp.sqrt(sums[2:3] / slot_total + EPSILON)
        rates.append((rate_keys, rate_values, rate_bias))
        if step < STEPS - 1:
            for s in range(2):
                part = slice(s * hs, (s + 1) * hs)
                kc[part] = keys[part] - rate_keys * og[step, y, s, 0]
                vc[part] = values[part] - rate_values * og[step, y, s, 1]
            whole = jnp.concatenate([ogb[step, y, 0, :1], ogb[step, y, 1, :1]], axis=1)
            bias_row = bias_row - rate_bias * whole

    for step in range(STEPS):
        for i in range(1, ny):
            other, dev = at_y(i)
            for s in (xh, 1 - xh):
                arrive(og.at[step, other, s], o_ss.at[step, other, s], o_rs.at[step, other, s], dev)
                arrive(ogb.at[step, other, s], ob_ss.at[step, other, s], ob_rs.at[step, other, s], dev)
    for h in range(ny):
        for s in range(2):
            part = slice(s * hs, (s + 1) * hs)
            new_keys, new_values, new_bias = k_in[h, part], v_in[h, part], b_in[h : h + 1, part]
            for step in range(STEPS):
                rate_keys, rate_values, rate_bias = rates[step]
                new_keys = new_keys - rate_keys * og[step, h, s, 0]
                new_values = new_values - rate_values * og[step, h, s, 1]
                new_bias = new_bias - rate_bias * ogb[step, h, s, :1]
            k_out[h, part] = new_keys
            v_out[h, part] = new_values
            b_out[h : h + 1, part] = new_bias
    for copy, when in pending:
        if when is None:
            copy.wait_send()
        else:
            pl.when(when)(copy.wait_send)


def per_device(nz, ny, nx, queries, compact_keys, compact_values, slot_bias, targets, positions, assignment):
    qb, d = queries.shape[1:]
    slots = compact_keys.shape[1]
    nb = ny // 2
    hq, dr, ng, hs = nb * qb, d // nz, ny * nx * 4, slots // 2
    sems = [(4,)]
    for shape in (
        (ny,), (ny,), (ny,), (STEPS, nb), (STEPS, nz), (STEPS, nb, nz), (STEPS, nz), (STEPS, nb, 2), (STEPS, 2),
        (STEPS, 2), (STEPS, ny, 2), (STEPS, ny, 2), (STEPS, ng), (STEPS, nz), (STEPS, nz),
    ):
        sems += [shape, shape]
    sems[16] = (STEPS, ny)
    buffers = [
        (ny, qb, d), (ny, slots, d), (ny, slots, d), (ny, qb, d),
        (ny, qb, d), (ny, qb, d), (ny, d, qb), (nb, dr, qb), (ny, 1, qb), (ny, 1, qb), (ny, slots, qb),
        (STEPS, ny, d + 8, qb), (STEPS, nb, d + 8, qb),
        (STEPS, nz, dr, hq), (STEPS, nz, dr, hq), (STEPS, hq // 128, 128), (STEPS, nz, hq // 128, 128),
        (STEPS, nb, dr, qb), (STEPS, ny, d, qb), (STEPS, ny + 1, nb, 1, qb),
        (STEPS, 2, 2, hs, d), (STEPS, 2, hs, d), (STEPS, 2, 8, hs), (STEPS, 8, hs),
        (STEPS, ny, 2, 2, hs, d), (STEPS, ny, 2, 8, hs),
        (STEPS, 8, 128), (STEPS, ng, 8, 128), (STEPS, 8, 128), (STEPS, nz, 8, 128),
        (slots, d), (slots, d),
    ]
    vmem, hbm = pl.BlockSpec(memory_space=pltpu.VMEM), pl.BlockSpec(memory_space=pl.ANY)
    return pl.pallas_call(
        functools.partial(kernel, nz, ny, nx),
        out_shape=tuple(pltpu.VMEM(x.shape, F32) for x in (compact_keys, compact_values, slot_bias)),
        in_specs=[hbm, hbm, hbm, vmem, hbm, vmem, pl.BlockSpec(memory_space=pltpu.SMEM)],
        out_specs=(vmem, vmem, vmem),
        scratch_shapes=[pltpu.VMEM(shape, F32) for shape in buffers]
        + [pltpu.SemaphoreType.DMA(shape) for shape in sems],
        compiler_params=pltpu.CompilerParams(collective_id=0, has_side_effects=True),
    )(queries, compact_keys, compact_values, slot_bias, targets, positions, assignment)


def solution(mesh):
    nz, ny, nx = mesh.shape["page"] // 2, mesh.shape["query"] // 2, mesh.shape["head"]
    placed = (
        P("head", "query", None),
        P("head", "page", None),
        P("head", "page", None),
        P("head", "page"),
        P("head", "query", None),
        P("head", "query"),
        P(),
    )
    return jax.shard_map(
        functools.partial(per_device, nz, ny, nx),
        mesh=mesh,
        in_specs=placed,
        out_specs=(P("head", "page", None), P("head", "page", None), P("head", "page")),
        check_vma=False,
    )
```

```python
import functools
import math

import jax
import jax.numpy as jnp
from jax import lax
from jax.experimental import pallas as pl
from jax.experimental.pallas import tpu as pltpu
from jax.sharding import PartitionSpec as P

STEPS = 2
PAGE_SHIFT = 15
MASKED = -1e30
EPSILON = 1e-06
RATE_KEYS = 0.05
RATE_VALUES = 0.05
RATE_BIAS = 0.2
HIGHEST = lax.Precision.HIGHEST
HIGH = lax.Precision.HIGH
MESH = pl.DeviceIdType.MESH
F32 = jnp.float32


def dot(a, b, ca, cb, precision=HIGH):
    return lax.dot_general(
        a, b, (((ca,), (cb,)), ((), ())), precision=precision, preferred_element_type=F32
    )


def pairs_of(nz):
    count = nz // 2
    far = sorted((o for o in range(count) if min(o, count - o) >= 2), key=lambda o: (-min(o, count - o), o))
    near = [(o, r) for o in sorted({0, 1 % count, count - 1}) for r in range(2) if o or r]
    return near, far


def far_first(n):
    return sorted(range(1, n), key=lambda i: (-min(i, n - i), i))


def kernel(
    nz, ny, nx, q_hbm, k_hbm, v_hbm, b_in, t_hbm, pos_in, page_in, k_out, v_out, b_out,
    q_in, k_in, v_in, t_in, qg, tq, tt, tp, pgs, pg, st_s, po, pin, zs, zr, zt, ztr, zfi, zfo, zft, rs, rt, lse,
    gl, gr, gbl, gbr, og, ogb, s1s, s1, s2s, s2, kc, vc,
    in_sem, q_ss, q_rs, t_ss, t_rs, g_ss, g_rs, c_ss, c_rs, z_ss, z_rs, a_ss, a_rs, f_ss, f_rs, l_ss, l_rs,
    p_ss, p_rs, h_ss, h_rs, o_ss, o_rs, ob_ss, ob_rs, s1_ss, s1_rs, s2_ss, s2_rs, y_ss, y_rs, x_ss, x_rs, w_ss, w_rs,
):
    qb, d = q_in.shape[1:]
    slots = k_in.shape[1]
    nb = ny // 2
    hq = nb * qb
    dr = d // nz
    kr = hq // 128
    ng = ny * nx * 4
    hs = slots // 2
    scale = 1.0 / math.sqrt(d)
    slot_total = ny * nx * slots * nz * 2
    entry_count = slot_total * d

    page = lax.axis_index("page")
    z, core = page // 2, lax.rem(page, 2)
    g = lax.axis_index("query")
    y, xh = g // 2, lax.rem(g, 2)
    xl = lax.axis_index("head")
    gi = (g * nx + xl) * 2 + core
    y_half, y_in = y // nb, lax.rem(y, nb)
    z_rows = pl.ds(pl.multiple_of(z * dr, dr), dr)
    near, far = pairs_of(nz)
    pz, zp = z // 2, lax.rem(z, 2)

    def at_pair(o, r):
        return lax.rem(pz + o, nz // 2) * 2 + lax.rem(zp + r, 2)

    mate = {"page": at_pair(0, 1) * 2 + core}
    arrivals = [(0, 0)] + near + [(o, 0) for o in far[::-1]] + [(o, 1) for o in far[::-1]]

    def at_z(i):
        other = lax.rem(z + i, nz)
        return other, {"page": other * 2 + core}

    def at_y(i):
        other = lax.rem(y + i, ny)
        return other, {"query": other * 2 + xh}

    def at_g(i):
        other = lax.rem(gi + i, ng)
        oc = lax.rem(other, 2)
        ox = lax.rem(other // 2, nx)
        return other, {"page": z * 2 + oc, "query": other // (2 * nx), "head": ox}

    def at_head(j, i):
        other = lax.rem(z + i, nz)
        return other, {"page": other * 2 + y_half, "query": (core * nb + j) * 2 + xh}

    other_core = {"page": z * 2 + 1 - core}
    pair = {"query": y * 2 + 1 - xh}

    loads = [
        pltpu.make_async_copy(src, dst, in_sem.at[n])
        for n, (src, dst) in enumerate(((q_hbm, q_in), (k_hbm, k_in), (v_hbm, v_in), (t_hbm, t_in)))
    ]
    for load in loads:
        load.start()

    barrier = pltpu.get_barrier_semaphore()
    for i in range(1, nz):
        for j in range(nb):
            pl.semaphore_signal(barrier, inc=1, device_id=at_head(j, i)[1], device_id_type=MESH)
        pl.semaphore_signal(barrier, inc=1, device_id=at_z(i)[1], device_id_type=MESH)
    for i in range(1, ng):
        pl.semaphore_signal(barrier, inc=1, device_id=at_g(i)[1], device_id_type=MESH)

    pending = []

    def send(src, dst, ss, rs_, dev, when=None):
        copy = pltpu.make_async_remote_copy(
            src_ref=src, dst_ref=dst, send_sem=ss, recv_sem=rs_, device_id=dev, device_id_type=MESH
        )
        if when is None:
            copy.start()
        else:
            pl.when(when)(copy.start)
        pending.append((copy, when))

    def arrive(dst, ss, rs_, dev, when=None):
        copy = pltpu.make_async_remote_copy(
            src_ref=dst, dst_ref=dst, send_sem=ss, recv_sem=rs_, device_id=dev, device_id_type=MESH
        )
        if when is None:
            copy.wait_recv()
        else:
            pl.when(when)(copy.wait_recv)

    def column(row):
        return jnp.transpose(jnp.broadcast_to(row, (128, slots)))[:, :1]

    def stack_rows(rows, height, width):
        at = lax.broadcasted_iota(jnp.int32, (height, width), 0)
        tile = jnp.zeros((height, width), F32)
        for r, row in enumerate(rows):
            tile = jnp.where(at == r, jnp.broadcast_to(row, (height, width)), tile)
        return tile

    def forward(step, blk, scores, seen, values):
        top = jnp.max(scores, axis=0, keepdims=True)
        weights = jnp.where(seen, jnp.exp(scores - top), 0.0)
        po[step, blk, :d, :] = dot(values, weights, 0, 0)
        total = jnp.sum(weights, axis=0, keepdims=True)
        po[step, blk, d:, :] = stack_rows([top, total], 8, qb)

    def share_core(step, j):
        c_ss_, c_rs_ = c_ss.at[step, j], c_rs.at[step, j]
        send(po.at[step, (1 - core) * nb + j], pin.at[step, j], c_ss_, c_rs_, other_core)

    my_page = page_in[page].astype(F32)
    pages = (pos_in[...] >> PAGE_SHIFT).astype(F32)
    for h in range(ny):
        pgs[h] = pages[h : h + 1]
    row_of = lax.broadcasted_iota(jnp.int32, (ny, slots), 0)

    def bias_of(h):
        return jnp.sum(jnp.where(row_of == h, b_in[...], 0.0), axis=0, keepdims=True)

    def first_forward(h):
        seen = my_page <= pgs[h]
        scores = dot(k_in[h], q_in[h], 1, 1, HIGHEST) * scale + column(bias_of(h))
        forward(0, h, jnp.where(seen, scores, MASKED), seen, v_in[h])

    for load in loads:
        load.wait()
    for j in range(nb):
        first_forward((1 - core) * nb + j)

    pl.semaphore_wait(barrier, (nz - 1) * (nb + 1) + ng - 1)

    for j in range(nb):
        share_core(0, j)
    for i in range(1, ny):
        other, dev = at_y(i)
        send(q_in.at[other], qg.at[y], q_ss.at[other], q_rs.at[y], dev)
        send(t_in.at[other], tq.at[y], t_ss.at[other], t_rs.at[y], dev)
        send(pgs.at[other], pg.at[y], g_ss.at[other], g_rs.at[y], dev)
    for j in range(nb):
        first_forward(core * nb + j)
    bias_row = bias_of(y)

    rates = []
    for step in range(STEPS):
        if step:
            keys, values = kc[...], vc[...]
            bias_col = column(bias_row)
            for n in range(ny):
                blk = (1 - core) * nb + n if n < nb else core * nb + n - nb
                seen = my_page <= pg[blk]
                scores = jnp.where(seen, dot(keys, qg[blk], 1, 1, HIGHEST) * scale + bias_col, MASKED)
                st_s[blk] = scores
                forward(step, blk, scores, seen, values)
                if n < nb:
                    share_core(step, n)

        stats = []
        for j in range(nb):
            arrive(pin.at[step, j], c_ss.at[step, j], c_rs.at[step, j], other_core)
            mine, theirs = po[step, core * nb + j], pin[step, j]
            m0, m1 = mine[d : d + 1], theirs[d : d + 1]
            top = jnp.maximum(m0, m1)
            f0, f1 = jnp.exp(m0 - top), jnp.exp(m1 - top)
            total = mine[d + 1 : d + 2] * f0 + theirs[d + 1 : d + 2] * f1
            some = total > 0.0
            inverse = jnp.where(some, 1.0 / jnp.where(some, total, 1.0), 0.0)
            merged = mine[:d] * (f0 * inverse) + theirs[:d] * (f1 * inverse)
            zs[step, :, :, j * qb : (j + 1) * qb] = merged.reshape(nz, dr, qb)
            chip = jnp.where(some, top + jnp.log(jnp.where(some, total, 1.0)), MASKED)
            stats += [chip[:, a : a + 128] for a in range(0, qb, 128)]
        tile = stack_rows(stats, kr, 128)
        zt[step] = tile

        for n, o in enumerate(far):
            send(zs.at[step, at_pair(o, 1)], zfi.at[step, n], x_ss.at[step, n], x_rs.at[step, n], mate)
        for n, (o, r) in enumerate(near):
            dev = {"page": at_pair(o, r) * 2 + core}
            send(zt.at[step], ztr.at[step, n], y_ss.at[step, n], y_rs.at[step, n], dev)
        mate_slot = near.index((0, 1))
        arrive(ztr.at[step, mate_slot], y_ss.at[step, mate_slot], y_rs.at[step, mate_slot], mate)
        theirs = ztr[step, mate_slot]
        top = jnp.maximum(tile, theirs)
        f0, f1 = jnp.exp(tile - top), jnp.exp(theirs - top)
        both = f0 + f1
        zft[step] = top + jnp.log(both)
        f0, f1 = f0 / both, f1 / both
        for n, o in enumerate(far):
            arrive(zfi.at[step, n], x_ss.at[step, n], x_rs.at[step, n], mate)
            other = at_pair(o, 0)
            for r in range(kr):
                lanes = slice(r * 128, (r + 1) * 128)
                mine, more = zs[step, other, :, lanes], zfi[step, n, :, lanes]
                zfo[step, n, :, lanes] = mine * f0[r : r + 1] + more * f1[r : r + 1]
            dev, slot = {"page": other * 2 + core}, len(near) + n
            send(zft.at[step], ztr.at[step, slot], y_ss.at[step, slot], y_rs.at[step, slot], dev)
            send(zfo.at[step, n], zr.at[step, slot], z_ss.at[step, slot], z_rs.at[step, slot], dev)
        for n, (o, r) in enumerate(near):
            other = at_pair(o, r)
            send(zs.at[step, other], zr.at[step, n], z_ss.at[step, n], z_rs.at[step, n], {"page": other * 2 + core})
        slots_in = len(near) + len(far)
        zr[step, slots_in] = zs[step, z]
        ztr[step, slots_in] = tile
        if step == 0:
            pick = (
                lax.broadcasted_iota(jnp.int32, (dr, d), 1)
                == lax.broadcasted_iota(jnp.int32, (dr, d), 0) + z * dr
            ).astype(F32)
            for j in range(nb):
                tp[j] = dot(pick, t_in[core * nb + j], 1, 1, HIGHEST)
            qg[y] = q_in[y]
            tq[y] = t_in[y]
            pg[y] = pgs[y]
            kc[...] = k_in[y]
            vc[...] = v_in[y]
            keys, values = kc[...], vc[...]
            bias_col = column(bias_row)
        if step == 0:
            for i in range(ny):
                blk, dev = at_y(i)
                if i:
                    arrive(qg.at[blk], q_ss.at[blk], q_rs.at[blk], dev)
                    arrive(tq.at[blk], t_ss.at[blk], t_rs.at[blk], dev)
                    arrive(pg.at[blk], g_ss.at[blk], g_rs.at[blk], dev)
                scores = dot(keys, qg[blk], 1, 1, HIGHEST) * scale + bias_col
                st_s[blk] = jnp.where(my_page <= pg[blk], scores, MASKED)
                tt[blk] = jnp.transpose(tq[blk])
        for n in range(slots_in):
            o, r = near[n] if n < len(near) else (far[n - len(near)], 0)
            dev = {"page": at_pair(o, r) * 2 + core}
            if n != mate_slot:
                arrive(ztr.at[step, n], y_ss.at[step, n], y_rs.at[step, n], dev)
            arrive(zr.at[step, n], z_ss.at[step, n], z_rs.at[step, n], dev)
        for r in range(kr):
            lanes = slice(r * 128, (r + 1) * 128)
            rows = [ztr[step, n, r : r + 1, :] for n in range(slots_in + 1)]
            top = functools.reduce(jnp.maximum, rows)
            shares = [jnp.exp(row - top) for row in rows]
            total = sum(shares[1:], shares[0])
            output = sum(zr[step, n, :, lanes] * share for n, share in enumerate(shares)) / total
            j, off = (r * 128) // qb, (r * 128) % qb
            blk = core * nb + j
            target = tp[j, :, off : off + 128] if step == 0 else tt[blk, z_rows, off : off + 128]
            rs[step, j, :, off : off + 128] = output - target
            lse[step, ny if step == 0 else blk, j, :, off : off + 128] = top + jnp.log(total)

        if step == 0:
            for j in range(nb):
                head = core * nb + j
                dev = at_head(j, 0)[1]
                away = head != y
                send(rs.at[0, j], rt.at[0, y, z_rows], a_ss.at[0, j, z], a_rs.at[0, y_in, z], dev, away)
                for c in range(2):
                    dev = {"page": z * 2 + c, "query": head * 2 + xh}
                    away = jnp.logical_or(head != y, core != c)
                    send(lse.at[0, ny, j], lse.at[0, y, 0], l_ss.at[0, j, c], l_rs.at[0, y], dev, away)

                @pl.when(head == y)
                def _(j=j):
                    rt[0, y, z_rows, :] = rs[0, j]
                    lse[0, y, 0] = lse[0, ny, j]

        for o, r in [(o, 0) for o in far] + near:
            other = at_pair(o, r)
            for j in range(nb):
                if step == 0:
                    blk, slot, dev = y, y_in, {"page": other * 2 + y_half, "query": (core * nb + j) * 2 + xh}
                else:
                    blk, slot, dev = core * nb + j, j, {"page": other * 2 + core}
                send(rs.at[step, j], rt.at[step, blk, z_rows], a_ss.at[step, j, other], a_rs.at[step, slot, z], dev)
        if step:
            for j in range(nb):
                rt[step, core * nb + j, z_rows, :] = rs[step, j]
                mine = lse.at[step, core * nb + j, j]
                send(mine, lse.at[step, core * nb + j, j], l_ss.at[step, j, 0], l_rs.at[step, core * nb + j], other_core)
        for n, (o, r) in enumerate(arrivals):
            other = at_pair(o, r)
            rows = pl.ds(pl.multiple_of(other * dr, dr), dr)
            there = rt.at[step, pl.ds(core * nb, nb), rows]
            if o in far and r:
                arrive(there, a_ss.at[step, 0, other], a_rs.at[step, 0, other], mate)
            elif n or step == 0:
                for j in range(nb):
                    blk = core * nb + j
                    dev = {"page": other * 2 + (core if step else y_half), "query": (y if step else blk) * 2 + xh}
                    when = blk != y if n == 0 else None
                    arrive(rt.at[step, blk, rows], a_ss.at[step, j, other], a_rs.at[step, j, other], dev, when)
            if o in far and not r:
                send(there, there, w_ss.at[step, other], a_rs.at[step, 0, other], mate)
            send(there, there, f_ss.at[step, other], f_rs.at[step, other], other_core)

        if step == 0:
            for blk in range(ny):
                when = jnp.logical_or(blk != y, y_half != core)
                dev = {"page": z * 2 + y_half, "query": blk * 2 + xh}
                arrive(lse.at[0, blk, 0], l_ss.at[0, 0, 0], l_rs.at[0, blk], dev, when)
        grad_keys = jnp.zeros((slots, d), F32)
        grad_values = jnp.zeros((slots, d), F32)
        grad_bias = jnp.zeros((8, slots), F32)
        for late in range(2):
            half = core if late == 0 else 1 - core
            if late:
                for o, r in arrivals:
                    other = at_pair(o, r)
                    rows = pl.ds(pl.multiple_of(other * dr, dr), dr)
                    there = rt.at[step, pl.ds(half * nb, nb), rows]
                    arrive(there, f_ss.at[step, other], f_rs.at[step, other], other_core)
                if step:
                    for j in range(nb):
                        blk = half * nb + j
                        arrive(lse.at[step, blk, j], l_ss.at[step, j, 0], l_rs.at[step, blk], other_core)
            for j in range(nb):
                blk = half * nb + j
                residual = rt[step, blk]
                delta = jnp.sum(residual * (residual + tt[blk]), axis=0, keepdims=True)
                attention = jnp.exp(st_s[blk] - lse[step, blk, j if step else 0])
                grad_values += dot(attention, residual, 1, 1)
                grad_scores = attention * (dot(values, residual, 1, 0) - delta)
                grad_keys += dot(grad_scores, qg[blk], 1, 0)
                grad_bias += dot(jnp.ones((8, qb), F32), grad_scores, 1, 1)
        for s in range(2):
            gl[step, s, 0] = grad_keys[s * hs : (s + 1) * hs] * scale
            gl[step, s, 1] = grad_values[s * hs : (s + 1) * hs]
            gbl[step, s] = grad_bias[:, s * hs : (s + 1) * hs]
        send(gl.at[step, 1 - xh], gr.at[step], p_ss.at[step, 0], p_rs.at[step, 0], pair)
        send(gbl.at[step, 1 - xh], gbr.at[step], p_ss.at[step, 1], p_rs.at[step, 1], pair)
        arrive(gr.at[step], p_ss.at[step, 0], p_rs.at[step, 0], pair)
        arrive(gbr.at[step], p_ss.at[step, 1], p_rs.at[step, 1], pair)
        grad_keys = gl[step, xh, 0] + gr[step, 0]
        grad_values = gl[step, xh, 1] + gr[step, 1]
        grad_bias = gbl[step, xh] + gbr[step]
        lane = lax.broadcasted_iota(jnp.int32, (1, 128), 1)
        row = jnp.zeros((1, 128), F32)
        for n, grad in enumerate((grad_keys, grad_values, grad_bias[:1])):
            square = jnp.sum(jnp.sum(grad * grad, axis=0, keepdims=True), axis=1, keepdims=True)
            row = jnp.where(lane == n, square, row)
        s1s[step] = row
        for i in range(1, ng):
            other, dev = at_g(i)
            send(s1s.at[step], s1.at[step, gi], s1_ss.at[step, other], s1_rs.at[step, gi], dev)
        s1[step, gi] = s1s[step]
        og[step, y, xh, 0] = grad_keys
        og[step, y, xh, 1] = grad_values
        ogb[step, y, xh] = grad_bias
        mine, mine_b = og.at[step, y, xh], ogb.at[step, y, xh]

        def gather(step=step, mine=mine, mine_b=mine_b):
            send(mine, mine, h_ss.at[step, 0], h_rs.at[step, 0], pair)
            send(mine_b, mine_b, h_ss.at[step, 1], h_rs.at[step, 1], pair)
            for i in range(1, ny):
                other, dev = at_y(i)
                send(mine, mine, o_ss.at[step, other, xh], o_rs.at[step, y, xh], dev)
                send(mine_b, mine_b, ob_ss.at[step, other, xh], ob_rs.at[step, y, xh], dev)

        if step == STEPS - 1:
            gather()
        for i in range(1, ng):
            other, dev = at_g(i)
            arrive(s1.at[step, other], s1_ss.at[step, other], s1_rs.at[step, other], dev)
        s2s[step] = jnp.sum(s1[step], axis=0)
        for i in far_first(nz):
            other, dev = at_z(i)
            send(s2s.at[step], s2.at[step, z], s2_ss.at[step, other], s2_rs.at[step, z], dev)
        s2[step, z] = s2s[step]
        if step < STEPS - 1:
            gather()
        theirs, theirs_b = og.at[step, y, 1 - xh], ogb.at[step, y, 1 - xh]
        arrive(theirs, h_ss.at[step, 0], h_rs.at[step, 0], pair)
        arrive(theirs_b, h_ss.at[step, 1], h_rs.at[step, 1], pair)
        for i in range(1, ny):
            other, dev = at_y(i)
            send(theirs, theirs, o_ss.at[step, other, 1 - xh], o_rs.at[step, y, 1 - xh], dev)
            send(theirs_b, theirs_b, ob_ss.at[step, other, 1 - xh], ob_rs.at[step, y, 1 - xh], dev)
        for i in range(1, nz):
            other, dev = at_z(i)
            arrive(s2.at[step, other], s2_ss.at[step, other], s2_rs.at[step, other], dev)
        row = jnp.sum(s2[step], axis=0)
        sums = [jnp.sum(jnp.where(lane == n, row, 0.0), axis=1, keepdims=True) for n in range(3)]
        rate_keys = RATE_KEYS / jnp.sqrt(sums[0] / entry_count + EPSILON)
        rate_values = RATE_VALUES / jnp.sqrt(sums[1] / entry_count + EPSILON)
        rate_bias = RATE_BIAS / jnp.sqrt(sums[2] / slot_total + EPSILON)
        rates.append((rate_keys, rate_values, rate_bias))
        if step < STEPS - 1:
            for s in range(2):
                part = slice(s * hs, (s + 1) * hs)
                kc[part] = keys[part] - rate_keys * og[step, y, s, 0]
                vc[part] = values[part] - rate_values * og[step, y, s, 1]
            whole = jnp.concatenate([ogb[step, y, 0, :1], ogb[step, y, 1, :1]], axis=1)
            bias_row = bias_row - rate_bias * whole

    for step in range(STEPS):
        for i in range(1, ny):
            other, dev = at_y(i)
            for s in (xh, 1 - xh):
                arrive(og.at[step, other, s], o_ss.at[step, other, s], o_rs.at[step, other, s], dev)
                arrive(ogb.at[step, other, s], ob_ss.at[step, other, s], ob_rs.at[step, other, s], dev)
    for h in range(ny):
        for s in range(2):
            part = slice(s * hs, (s + 1) * hs)
            new_keys, new_values, new_bias = k_in[h, part], v_in[h, part], b_in[h : h + 1, part]
            for step in range(STEPS):
                rate_keys, rate_values, rate_bias = rates[step]
                new_keys = new_keys - rate_keys * og[step, h, s, 0]
                new_values = new_values - rate_values * og[step, h, s, 1]
                new_bias = new_bias - rate_bias * ogb[step, h, s, :1]
            k_out[h, part] = new_keys
            v_out[h, part] = new_values
            b_out[h : h + 1, part] = new_bias
    for copy, when in pending:
        if when is None:
            copy.wait_send()
        else:
            pl.when(when)(copy.wait_send)


def per_device(nz, ny, nx, queries, compact_keys, compact_values, slot_bias, targets, positions, assignment):
    qb, d = queries.shape[1:]
    slots = compact_keys.shape[1]
    nb = ny // 2
    hq, dr, ng, hs = nb * qb, d // nz, ny * nx * 4, slots // 2
    near, far = pairs_of(nz)
    ins, nf, kr = len(near) + len(far) + 1, max(len(far), 1), hq // 128
    sems = [(4,)]
    for shape in (
        (ny,), (ny,), (ny,), (STEPS, nb), (STEPS, ins), (STEPS, nb, nz), (STEPS, nz), (STEPS, nb, 2), (STEPS, 2),
        (STEPS, 2), (STEPS, ny, 2), (STEPS, ny, 2), (STEPS, ng), (STEPS, nz), (STEPS, ins), (STEPS, nf), (STEPS, nz),
    ):
        sems += [shape, shape]
    sems[16] = (STEPS, ny)
    buffers = [
        (ny, qb, d), (ny, slots, d), (ny, slots, d), (ny, qb, d),
        (ny, qb, d), (ny, qb, d), (ny, d, qb), (nb, dr, qb), (ny, 1, qb), (ny, 1, qb), (ny, slots, qb),
        (STEPS, ny, d + 8, qb), (STEPS, nb, d + 8, qb),
        (STEPS, nz, dr, hq), (STEPS, ins, dr, hq), (STEPS, kr, 128), (STEPS, ins, kr, 128),
        (STEPS, nf, dr, hq), (STEPS, nf, dr, hq), (STEPS, kr, 128),
        (STEPS, nb, dr, qb), (STEPS, ny, d, qb), (STEPS, ny + 1, nb, 1, qb),
        (STEPS, 2, 2, hs, d), (STEPS, 2, hs, d), (STEPS, 2, 8, hs), (STEPS, 8, hs),
        (STEPS, ny, 2, 2, hs, d), (STEPS, ny, 2, 8, hs),
        (STEPS, 1, 128), (STEPS, ng, 1, 128), (STEPS, 1, 128), (STEPS, nz, 1, 128),
        (slots, d), (slots, d),
    ]
    vmem, hbm = pl.BlockSpec(memory_space=pltpu.VMEM), pl.BlockSpec(memory_space=pl.ANY)
    return pl.pallas_call(
        functools.partial(kernel, nz, ny, nx),
        out_shape=tuple(pltpu.VMEM(x.shape, F32) for x in (compact_keys, compact_values, slot_bias)),
        in_specs=[hbm, hbm, hbm, vmem, hbm, vmem, pl.BlockSpec(memory_space=pltpu.SMEM)],
        out_specs=(vmem, vmem, vmem),
        scratch_shapes=[pltpu.VMEM(shape, F32) for shape in buffers]
        + [pltpu.SemaphoreType.DMA(shape) for shape in sems],
        compiler_params=pltpu.CompilerParams(collective_id=0, has_side_effects=True),
    )(queries, compact_keys, compact_values, slot_bias, targets, positions, assignment)


def solution(mesh):
    nz, ny, nx = mesh.shape["page"] // 2, mesh.shape["query"] // 2, mesh.shape["head"]
    placed = (
        P("head", "query", None),
        P("head", "page", None),
        P("head", "page", None),
        P("head", "page"),
        P("head", "query", None),
        P("head", "query"),
        P(),
    )
    return jax.shard_map(
        functools.partial(per_device, nz, ny, nx),
        mesh=mesh,
        in_specs=placed,
        out_specs=(P("head", "page", None), P("head", "page", None), P("head", "page")),
        check_vma=False,
    )
```

```python
import functools
import math

import jax
import jax.numpy as jnp
from jax import lax
from jax.experimental import pallas as pl
from jax.experimental.pallas import tpu as pltpu
from jax.sharding import PartitionSpec as P

STEPS = 2
PAGE_SHIFT = 15
MASKED = -1e30
EPSILON = 1e-06
RATE_KEYS = 0.05
RATE_VALUES = 0.05
RATE_BIAS = 0.2
HIGHEST = lax.Precision.HIGHEST
HIGH = lax.Precision.HIGH
MESH = pl.DeviceIdType.MESH
F32 = jnp.float32


def dot(a, b, ca, cb, precision=HIGH):
    return lax.dot_general(
        a, b, (((ca,), (cb,)), ((), ())), precision=precision, preferred_element_type=F32
    )


def pairs_of(nz):
    count = nz // 2
    far = sorted((o for o in range(count) if min(o, count - o) >= 2), key=lambda o: (-min(o, count - o), o))
    near = [(o, r) for o in sorted({0, 1 % count, count - 1}) for r in range(2) if o or r]
    return near, far


def far_first(n):
    return sorted(range(1, n), key=lambda i: (-min(i, n - i), i))


def kernel(
    nz, ny, nx, q_hbm, k_hbm, v_hbm, b_in, t_hbm, pos_in, page_in, k_out, v_out, b_out,
    q_in, k_in, v_in, t_in, qg, tq, tt, tp, pgs, pg, st_s, po, pin, zs, zr, zt, ztr, zfi, zfo, zft, rs, rt, lse,
    gl, gr, gbl, gbr, og, ogb, s1s, s1, s2s, s2, pk, vc,
    in_sem, q_ss, q_rs, t_ss, t_rs, g_ss, g_rs, c_ss, c_rs, z_ss, z_rs, a_ss, a_rs, f_ss, f_rs, l_ss, l_rs,
    p_ss, p_rs, h_ss, h_rs, o_ss, o_rs, ob_ss, ob_rs, s1_ss, s1_rs, s2_ss, s2_rs, y_ss, y_rs, x_ss, x_rs, w_ss, w_rs,
):
    qb, d = q_in.shape[1:]
    slots = k_in.shape[1]
    nb = ny // 2
    hq = nb * qb
    dr = d // nz
    kr = hq // 128
    ng = ny * nx * 4
    hs = slots // 2
    scale = 1.0 / math.sqrt(d)
    slot_total = ny * nx * slots * nz * 2
    entry_count = slot_total * d

    page = lax.axis_index("page")
    z, core = page // 2, lax.rem(page, 2)
    g = lax.axis_index("query")
    y, xh = g // 2, lax.rem(g, 2)
    xl = lax.axis_index("head")
    gi = (g * nx + xl) * 2 + core
    y_half, y_in = y // nb, lax.rem(y, nb)
    z_rows = pl.ds(pl.multiple_of(z * dr, dr), dr)
    near, far = pairs_of(nz)
    pz, zp = z // 2, lax.rem(z, 2)

    def at_pair(o, r):
        return lax.rem(pz + o, nz // 2) * 2 + lax.rem(zp + r, 2)

    mate = {"page": at_pair(0, 1) * 2 + core}
    arrivals = [(0, 0)] + near + [(o, 0) for o in far[::-1]] + [(o, 1) for o in far[::-1]]

    def at_z(i):
        other = lax.rem(z + i, nz)
        return other, {"page": other * 2 + core}

    def at_y(i):
        other = lax.rem(y + i, ny)
        return other, {"query": other * 2 + xh}

    def at_g(i):
        other = lax.rem(gi + i, ng)
        oc = lax.rem(other, 2)
        ox = lax.rem(other // 2, nx)
        return other, {"page": z * 2 + oc, "query": other // (2 * nx), "head": ox}

    def at_head(j, i):
        other = lax.rem(z + i, nz)
        return other, {"page": other * 2 + y_half, "query": (core * nb + j) * 2 + xh}

    other_core = {"page": z * 2 + 1 - core}
    pair = {"query": y * 2 + 1 - xh}

    loads = [
        pltpu.make_async_copy(src, dst, in_sem.at[n])
        for n, (src, dst) in enumerate(((q_hbm, q_in), (k_hbm, k_in), (v_hbm, v_in), (t_hbm, t_in)))
    ]
    for load in loads:
        load.start()

    barrier = pltpu.get_barrier_semaphore()
    for i in range(1, nz):
        for j in range(nb):
            pl.semaphore_signal(barrier, inc=1, device_id=at_head(j, i)[1], device_id_type=MESH)
        pl.semaphore_signal(barrier, inc=1, device_id=at_z(i)[1], device_id_type=MESH)
    for i in range(1, ng):
        pl.semaphore_signal(barrier, inc=1, device_id=at_g(i)[1], device_id_type=MESH)

    pending = []

    def send(src, dst, ss, rs_, dev, when=None):
        copy = pltpu.make_async_remote_copy(
            src_ref=src, dst_ref=dst, send_sem=ss, recv_sem=rs_, device_id=dev, device_id_type=MESH
        )
        if when is None:
            copy.start()
        else:
            pl.when(when)(copy.start)
        pending.append((copy, when))

    def arrive(dst, ss, rs_, dev, when=None):
        copy = pltpu.make_async_remote_copy(
            src_ref=dst, dst_ref=dst, send_sem=ss, recv_sem=rs_, device_id=dev, device_id_type=MESH
        )
        if when is None:
            copy.wait_recv()
        else:
            pl.when(when)(copy.wait_recv)

    def column(row):
        return jnp.transpose(jnp.broadcast_to(row, (128, slots)))[:, :1]

    def stack_rows(rows, height, width):
        at = lax.broadcasted_iota(jnp.int32, (height, width), 0)
        tile = jnp.zeros((height, width), F32)
        for r, row in enumerate(rows):
            tile = jnp.where(at == r, jnp.broadcast_to(row, (height, width)), tile)
        return tile

    def forward(step, blk, scores, seen, values):
        top = jnp.max(scores, axis=0, keepdims=True)
        weights = jnp.where(seen, jnp.exp(scores - top), 0.0)
        po[step, blk, :d, :] = dot(values, weights, 0, 0)
        total = jnp.sum(weights, axis=0, keepdims=True)
        po[step, blk, d:, :] = stack_rows([top, total], 8, qb)

    def share_core(step, j):
        c_ss_, c_rs_ = c_ss.at[step, j], c_rs.at[step, j]
        send(po.at[step, (1 - core) * nb + j], pin.at[step, j], c_ss_, c_rs_, other_core)

    my_page = page_in[page].astype(F32)
    pages = (pos_in[...] >> PAGE_SHIFT).astype(F32)
    for h in range(ny):
        pgs[h] = pages[h : h + 1]
    row_of = lax.broadcasted_iota(jnp.int32, (ny, slots), 0)

    def bias_of(h):
        return jnp.sum(jnp.where(row_of == h, b_in[...], 0.0), axis=0, keepdims=True)

    def first_forward(h):
        seen = my_page <= pgs[h]
        scores = dot(k_in[h], q_in[h], 1, 1, HIGHEST) * scale + column(bias_of(h))
        forward(0, h, jnp.where(seen, scores, MASKED), seen, v_in[h])

    for load in loads:
        load.wait()
    for j in range(nb):
        first_forward((1 - core) * nb + j)

    pl.semaphore_wait(barrier, (nz - 1) * (nb + 1) + ng - 1)

    for j in range(nb):
        share_core(0, j)
    for i in range(1, ny):
        other, dev = at_y(i)
        send(q_in.at[other], qg.at[y], q_ss.at[other], q_rs.at[y], dev)
        send(t_in.at[other], tq.at[y], t_ss.at[other], t_rs.at[y], dev)
        send(pgs.at[other], pg.at[y], g_ss.at[other], g_rs.at[y], dev)
    for j in range(nb):
        first_forward(core * nb + j)
    bias_row = bias_of(y)

    rates = []

    def arrive_slots(step):
        for i in range(1, ny):
            other, dev = at_y(i)
            for s in (xh, 1 - xh):
                arrive(og.at[step, other, s], o_ss.at[step, other, s], o_rs.at[step, other, s], dev)
                arrive(ogb.at[step, other, s], ob_ss.at[step, other, s], ob_rs.at[step, other, s], dev)

    def update_slots(step):
        rate_keys, rate_values, rate_bias = rates[step]
        for h in range(ny):
            for s in range(2):
                part = slice(s * hs, (s + 1) * hs)
                old = (k_out, v_out, b_out) if step else (k_in, v_in, b_in)
                k_out[h, part] = old[0][h, part] - rate_keys * og[step, h, s, 0]
                v_out[h, part] = old[1][h, part] - rate_values * og[step, h, s, 1]
                b_out[h : h + 1, part] = old[2][h : h + 1, part] - rate_bias * ogb[step, h, s, :1]

    for step in range(STEPS):
        if step:
            values = vc[...]
            rate_scores, step_bias = rates[-1][0] * scale, rates[-1][2] * bias_grad_col
            for n in range(ny):
                blk = (1 - core) * nb + n if n < nb else core * nb + n - nb
                seen = my_page <= pg[blk]
                scores = jnp.where(seen, st_s[blk] - rate_scores * pk[blk] - step_bias, MASKED)
                st_s[blk] = scores
                forward(step, blk, scores, seen, values)
                if n < nb:
                    share_core(step, n)

        stats = []
        for j in range(nb):
            arrive(pin.at[step, j], c_ss.at[step, j], c_rs.at[step, j], other_core)
            mine, theirs = po[step, core * nb + j], pin[step, j]
            m0, m1 = mine[d : d + 1], theirs[d : d + 1]
            top = jnp.maximum(m0, m1)
            f0, f1 = jnp.exp(m0 - top), jnp.exp(m1 - top)
            total = mine[d + 1 : d + 2] * f0 + theirs[d + 1 : d + 2] * f1
            some = total > 0.0
            inverse = jnp.where(some, 1.0 / jnp.where(some, total, 1.0), 0.0)
            merged = mine[:d] * (f0 * inverse) + theirs[:d] * (f1 * inverse)
            zs[step, :, :, j * qb : (j + 1) * qb] = merged.reshape(nz, dr, qb)
            chip = jnp.where(some, top + jnp.log(jnp.where(some, total, 1.0)), MASKED)
            stats += [chip[:, a : a + 128] for a in range(0, qb, 128)]
        tile = stack_rows(stats, kr, 128)
        zt[step] = tile

        for n, o in enumerate(far):
            send(zs.at[step, at_pair(o, 1)], zfi.at[step, n], x_ss.at[step, n], x_rs.at[step, n], mate)
        for n, (o, r) in enumerate(near):
            dev = {"page": at_pair(o, r) * 2 + core}
            send(zt.at[step], ztr.at[step, n], y_ss.at[step, n], y_rs.at[step, n], dev)
        for n, (o, r) in enumerate(near):
            other = at_pair(o, r)
            send(zs.at[step, other], zr.at[step, n], z_ss.at[step, n], z_rs.at[step, n], {"page": other * 2 + core})
        mate_slot = near.index((0, 1))
        arrive(ztr.at[step, mate_slot], y_ss.at[step, mate_slot], y_rs.at[step, mate_slot], mate)
        theirs = ztr[step, mate_slot]
        top = jnp.maximum(tile, theirs)
        f0, f1 = jnp.exp(tile - top), jnp.exp(theirs - top)
        both = f0 + f1
        zft[step] = top + jnp.log(both)
        f0, f1 = f0 / both, f1 / both
        for n, o in enumerate(far):
            arrive(zfi.at[step, n], x_ss.at[step, n], x_rs.at[step, n], mate)
            other = at_pair(o, 0)
            for r in range(kr):
                lanes = slice(r * 128, (r + 1) * 128)
                mine, more = zs[step, other, :, lanes], zfi[step, n, :, lanes]
                zfo[step, n, :, lanes] = mine * f0[r : r + 1] + more * f1[r : r + 1]
            dev, slot = {"page": other * 2 + core}, len(near) + n
            send(zft.at[step], ztr.at[step, slot], y_ss.at[step, slot], y_rs.at[step, slot], dev)
            send(zfo.at[step, n], zr.at[step, slot], z_ss.at[step, slot], z_rs.at[step, slot], dev)
        if step:
            arrive_slots(step - 1)
            update_slots(step - 1)
        slots_in = len(near) + len(far)
        zr[step, slots_in] = zs[step, z]
        ztr[step, slots_in] = tile
        if step == 0:
            pick = (
                lax.broadcasted_iota(jnp.int32, (dr, d), 1)
                == lax.broadcasted_iota(jnp.int32, (dr, d), 0) + z * dr
            ).astype(F32)
            for j in range(nb):
                tp[j] = dot(pick, t_in[core * nb + j], 1, 1, HIGHEST)
            qg[y] = q_in[y]
            tq[y] = t_in[y]
            pg[y] = pgs[y]
            keys, values = k_in[y], v_in[y]
            bias_col = column(bias_row)
        if step == 0:
            for i in range(ny):
                blk, dev = at_y(i)
                if i:
                    arrive(qg.at[blk], q_ss.at[blk], q_rs.at[blk], dev)
                    arrive(tq.at[blk], t_ss.at[blk], t_rs.at[blk], dev)
                    arrive(pg.at[blk], g_ss.at[blk], g_rs.at[blk], dev)
                scores = dot(keys, qg[blk], 1, 1, HIGHEST) * scale + bias_col
                st_s[blk] = jnp.where(my_page <= pg[blk], scores, MASKED)
                tt[blk] = jnp.transpose(tq[blk])
        for n in range(slots_in):
            o, r = near[n] if n < len(near) else (far[n - len(near)], 0)
            dev = {"page": at_pair(o, r) * 2 + core}
            if n != mate_slot:
                arrive(ztr.at[step, n], y_ss.at[step, n], y_rs.at[step, n], dev)
            arrive(zr.at[step, n], z_ss.at[step, n], z_rs.at[step, n], dev)
        for r in range(kr):
            lanes = slice(r * 128, (r + 1) * 128)
            rows = [ztr[step, n, r : r + 1, :] for n in range(slots_in + 1)]
            top = functools.reduce(jnp.maximum, rows)
            shares = [jnp.exp(row - top) for row in rows]
            total = sum(shares[1:], shares[0])
            output = sum(zr[step, n, :, lanes] * share for n, share in enumerate(shares)) / total
            j, off = (r * 128) // qb, (r * 128) % qb
            blk = core * nb + j
            target = tp[j, :, off : off + 128] if step == 0 else tt[blk, z_rows, off : off + 128]
            rs[step, j, :, off : off + 128] = output - target
            lse[step, ny if step == 0 else blk, j, :, off : off + 128] = top + jnp.log(total)

        if step == 0:
            for j in range(nb):
                head = core * nb + j
                dev = at_head(j, 0)[1]
                away = head != y
                send(rs.at[0, j], rt.at[0, y, z_rows], a_ss.at[0, j, z], a_rs.at[0, y_in, z], dev, away)
                for c in range(2):
                    dev = {"page": z * 2 + c, "query": head * 2 + xh}
                    away = jnp.logical_or(head != y, core != c)
                    send(lse.at[0, ny, j], lse.at[0, y, 0], l_ss.at[0, j, c], l_rs.at[0, y], dev, away)

                @pl.when(head == y)
                def _(j=j):
                    rt[0, y, z_rows, :] = rs[0, j]
                    lse[0, y, 0] = lse[0, ny, j]

        for o, r in [(o, 0) for o in far] + near:
            other = at_pair(o, r)
            for j in range(nb):
                if step == 0:
                    blk, slot, dev = y, y_in, {"page": other * 2 + y_half, "query": (core * nb + j) * 2 + xh}
                else:
                    blk, slot, dev = core * nb + j, j, {"page": other * 2 + core}
                send(rs.at[step, j], rt.at[step, blk, z_rows], a_ss.at[step, j, other], a_rs.at[step, slot, z], dev)
        if step:
            for j in range(nb):
                rt[step, core * nb + j, z_rows, :] = rs[step, j]
                mine = lse.at[step, core * nb + j, j]
                send(mine, lse.at[step, core * nb + j, j], l_ss.at[step, j, 0], l_rs.at[step, core * nb + j], other_core)
        for n, (o, r) in enumerate(arrivals):
            other = at_pair(o, r)
            rows = pl.ds(pl.multiple_of(other * dr, dr), dr)
            there = rt.at[step, pl.ds(core * nb, nb), rows]
            if o in far and r:
                arrive(there, a_ss.at[step, 0, other], a_rs.at[step, 0, other], mate)
            elif n or step == 0:
                for j in range(nb):
                    blk = core * nb + j
                    dev = {"page": other * 2 + (core if step else y_half), "query": (y if step else blk) * 2 + xh}
                    when = blk != y if n == 0 else None
                    arrive(rt.at[step, blk, rows], a_ss.at[step, j, other], a_rs.at[step, j, other], dev, when)
            if o in far and not r:
                send(there, there, w_ss.at[step, other], a_rs.at[step, 0, other], mate)
            send(there, there, f_ss.at[step, other], f_rs.at[step, other], other_core)

        if step == 0:
            for blk in range(ny):
                when = jnp.logical_or(blk != y, y_half != core)
                dev = {"page": z * 2 + y_half, "query": blk * 2 + xh}
                arrive(lse.at[0, blk, 0], l_ss.at[0, 0, 0], l_rs.at[0, blk], dev, when)
        grad_keys = jnp.zeros((slots, d), F32)
        grad_values = jnp.zeros((slots, d), F32)
        grad_bias = jnp.zeros((8, slots), F32)
        for late in range(2):
            half = core if late == 0 else 1 - core
            if late:
                for o, r in arrivals:
                    other = at_pair(o, r)
                    rows = pl.ds(pl.multiple_of(other * dr, dr), dr)
                    there = rt.at[step, pl.ds(half * nb, nb), rows]
                    arrive(there, f_ss.at[step, other], f_rs.at[step, other], other_core)
                if step:
                    for j in range(nb):
                        blk = half * nb + j
                        arrive(lse.at[step, blk, j], l_ss.at[step, j, 0], l_rs.at[step, blk], other_core)
            for j in range(nb):
                blk = half * nb + j
                residual = rt[step, blk]
                delta = jnp.sum(residual * (residual + tt[blk]), axis=0, keepdims=True)
                attention = jnp.exp(st_s[blk] - lse[step, blk, j if step else 0])
                grad_values += dot(attention, residual, 1, 1)
                grad_scores = attention * (dot(values, residual, 1, 0) - delta)
                grad_keys += dot(grad_scores, qg[blk], 1, 0)
                grad_bias += dot(jnp.ones((8, qb), F32), grad_scores, 1, 1)
        for s in range(2):
            gl[step, s, 0] = grad_keys[s * hs : (s + 1) * hs] * scale
            gl[step, s, 1] = grad_values[s * hs : (s + 1) * hs]
            gbl[step, s] = grad_bias[:, s * hs : (s + 1) * hs]
        send(gl.at[step, 1 - xh], gr.at[step], p_ss.at[step, 0], p_rs.at[step, 0], pair)
        send(gbl.at[step, 1 - xh], gbr.at[step], p_ss.at[step, 1], p_rs.at[step, 1], pair)
        arrive(gr.at[step], p_ss.at[step, 0], p_rs.at[step, 0], pair)
        arrive(gbr.at[step], p_ss.at[step, 1], p_rs.at[step, 1], pair)
        grad_keys = gl[step, xh, 0] + gr[step, 0]
        grad_values = gl[step, xh, 1] + gr[step, 1]
        grad_bias = gbl[step, xh] + gbr[step]
        lane = lax.broadcasted_iota(jnp.int32, (1, 128), 1)
        row = jnp.zeros((1, 128), F32)
        for n, grad in enumerate((grad_keys, grad_values, grad_bias[:1])):
            square = jnp.sum(jnp.sum(grad * grad, axis=0, keepdims=True), axis=1, keepdims=True)
            row = jnp.where(lane == n, square, row)
        s1s[step] = row
        for i in range(1, ng):
            other, dev = at_g(i)
            send(s1s.at[step], s1.at[step, gi], s1_ss.at[step, other], s1_rs.at[step, gi], dev)
        s1[step, gi] = s1s[step]
        og[step, y, xh, 0] = grad_keys
        og[step, y, xh, 1] = grad_values
        ogb[step, y, xh] = grad_bias
        mine, mine_b = og.at[step, y, xh], ogb.at[step, y, xh]

        def gather(step=step, mine=mine, mine_b=mine_b):
            send(mine, mine, h_ss.at[step, 0], h_rs.at[step, 0], pair)
            send(mine_b, mine_b, h_ss.at[step, 1], h_rs.at[step, 1], pair)
            for i in range(1, ny):
                other, dev = at_y(i)
                send(mine, mine, o_ss.at[step, other, xh], o_rs.at[step, y, xh], dev)
                send(mine_b, mine_b, ob_ss.at[step, other, xh], ob_rs.at[step, y, xh], dev)

        if step == STEPS - 1:
            gather()
        for i in range(1, ng):
            other, dev = at_g(i)
            arrive(s1.at[step, other], s1_ss.at[step, other], s1_rs.at[step, other], dev)
        s2s[step] = jnp.sum(s1[step], axis=0)
        for i in far_first(nz):
            other, dev = at_z(i)
            send(s2s.at[step], s2.at[step, z], s2_ss.at[step, other], s2_rs.at[step, z], dev)
        s2[step, z] = s2s[step]
        if step < STEPS - 1:
            gather()

        def products(s, step=step):
            rows = pl.ds(pl.multiple_of(s * hs, hs), hs)
            for blk in range(ny):
                pk[blk, rows, :] = dot(og[step, y, s, 0], qg[blk], 1, 1, HIGHEST)

        if step < STEPS - 1:
            products(xh)
        theirs, theirs_b = og.at[step, y, 1 - xh], ogb.at[step, y, 1 - xh]
        arrive(theirs, h_ss.at[step, 0], h_rs.at[step, 0], pair)
        arrive(theirs_b, h_ss.at[step, 1], h_rs.at[step, 1], pair)
        for i in range(1, ny):
            other, dev = at_y(i)
            send(theirs, theirs, o_ss.at[step, other, 1 - xh], o_rs.at[step, y, 1 - xh], dev)
            send(theirs_b, theirs_b, ob_ss.at[step, other, 1 - xh], ob_rs.at[step, y, 1 - xh], dev)
        if step < STEPS - 1:
            products(1 - xh)
            bias_grad_col = column(jnp.concatenate([ogb[step, y, 0, :1], ogb[step, y, 1, :1]], axis=1))
        for i in range(1, nz):
            other, dev = at_z(i)
            arrive(s2.at[step, other], s2_ss.at[step, other], s2_rs.at[step, other], dev)
        row = jnp.sum(s2[step], axis=0)
        sums = [jnp.sum(jnp.where(lane == n, row, 0.0), axis=1, keepdims=True) for n in range(3)]
        rate_keys = RATE_KEYS / jnp.sqrt(sums[0] / entry_count + EPSILON)
        rate_values = RATE_VALUES / jnp.sqrt(sums[1] / entry_count + EPSILON)
        rate_bias = RATE_BIAS / jnp.sqrt(sums[2] / slot_total + EPSILON)
        rates.append((rate_keys, rate_values, rate_bias))
        if step < STEPS - 1:
            for s in range(2):
                part = slice(s * hs, (s + 1) * hs)
                vc[part] = values[part] - rate_values * og[step, y, s, 1]

    arrive_slots(STEPS - 1)
    update_slots(STEPS - 1)
    for copy, when in pending:
        if when is None:
            copy.wait_send()
        else:
            pl.when(when)(copy.wait_send)


def per_device(nz, ny, nx, queries, compact_keys, compact_values, slot_bias, targets, positions, assignment):
    qb, d = queries.shape[1:]
    slots = compact_keys.shape[1]
    nb = ny // 2
    hq, dr, ng, hs = nb * qb, d // nz, ny * nx * 4, slots // 2
    near, far = pairs_of(nz)
    ins, nf, kr = len(near) + len(far) + 1, max(len(far), 1), hq // 128
    sems = [(4,)]
    for shape in (
        (ny,), (ny,), (ny,), (STEPS, nb), (STEPS, ins), (STEPS, nb, nz), (STEPS, nz), (STEPS, nb, 2), (STEPS, 2),
        (STEPS, 2), (STEPS, ny, 2), (STEPS, ny, 2), (STEPS, ng), (STEPS, nz), (STEPS, ins), (STEPS, nf), (STEPS, nz),
    ):
        sems += [shape, shape]
    sems[16] = (STEPS, ny)
    buffers = [
        (ny, qb, d), (ny, slots, d), (ny, slots, d), (ny, qb, d),
        (ny, qb, d), (ny, qb, d), (ny, d, qb), (nb, dr, qb), (ny, 1, qb), (ny, 1, qb), (ny, slots, qb),
        (STEPS, ny, d + 8, qb), (STEPS, nb, d + 8, qb),
        (STEPS, nz, dr, hq), (STEPS, ins, dr, hq), (STEPS, kr, 128), (STEPS, ins, kr, 128),
        (STEPS, nf, dr, hq), (STEPS, nf, dr, hq), (STEPS, kr, 128),
        (STEPS, nb, dr, qb), (STEPS, ny, d, qb), (STEPS, ny + 1, nb, 1, qb),
        (STEPS, 2, 2, hs, d), (STEPS, 2, hs, d), (STEPS, 2, 8, hs), (STEPS, 8, hs),
        (STEPS, ny, 2, 2, hs, d), (STEPS, ny, 2, 8, hs),
        (STEPS, 1, 128), (STEPS, ng, 1, 128), (STEPS, 1, 128), (STEPS, nz, 1, 128),
        (ny, slots, qb), (slots, d),
    ]
    vmem, hbm = pl.BlockSpec(memory_space=pltpu.VMEM), pl.BlockSpec(memory_space=pl.ANY)
    return pl.pallas_call(
        functools.partial(kernel, nz, ny, nx),
        out_shape=tuple(pltpu.VMEM(x.shape, F32) for x in (compact_keys, compact_values, slot_bias)),
        in_specs=[hbm, hbm, hbm, vmem, hbm, vmem, pl.BlockSpec(memory_space=pltpu.SMEM)],
        out_specs=(vmem, vmem, vmem),
        scratch_shapes=[pltpu.VMEM(shape, F32) for shape in buffers]
        + [pltpu.SemaphoreType.DMA(shape) for shape in sems],
        compiler_params=pltpu.CompilerParams(collective_id=0, has_side_effects=True),
    )(queries, compact_keys, compact_values, slot_bias, targets, positions, assignment)


def solution(mesh):
    nz, ny, nx = mesh.shape["page"] // 2, mesh.shape["query"] // 2, mesh.shape["head"]
    placed = (
        P("head", "query", None),
        P("head", "page", None),
        P("head", "page", None),
        P("head", "page"),
        P("head", "query", None),
        P("head", "query"),
        P(),
    )
    return jax.shard_map(
        functools.partial(per_device, nz, ny, nx),
        mesh=mesh,
        in_specs=placed,
        out_specs=(P("head", "page", None), P("head", "page", None), P("head", "page")),
        check_vma=False,
    )
```
